512 devices in a mesh: ops: 32 (over y_lo, x, core), sec: 16 (over y_hi, z).
Axes of the slice: x: 4, y: 8 (y_hi: 2, y_lo: 4; y = y_hi * 4 + y_lo), z: 8, core: 2. Of those that a mesh axis runs over, the one named last changes fastest.
Arguments:
- wavefunction: float32 [32, 128, 128], P('sec'), may hold values from -6 to 6
- hamiltonian_diag: float32 [32, 128, 128], P('sec'), may hold values from -6 to 6
- mirror_coupling: float32 [32], P('sec'), may hold values from 0.5 to 1.5, as said below
- left_env: float32 [768, 32, 128, 128], P('ops', 'sec'), as said below
- right_env: float32 [768, 128, 128], P('ops'), as said below
- term_source: int32 [768, 32], P('ops', 'sec'), may hold values from -1 to 31, as said below
Outputs:
- new_wave: float32 [32, 128, 128], P('sec', 'ops')
- new_sigma: float32 [32, 128, 128], P('sec', 'ops')
- energy: float32 [1], replicated
The draws below stay inside these ranges and needn't reach their ends.
Inputs may be any that keep to these rules, and one draw needn't show every extreme that they name: `term_source`: for each term the non-negative entries over the 32 target sectors are distinct; terms 0 and 1 have a block for every sector; for even k, term k + 1 maps sector t into sector s exactly where term k maps s into t. For even k and term_source[k, s] = t >= 0, left_env[k + 1, t] is the transpose of left_env[k, s]. For even k, right_env[k + 1] is the transpose of right_env[k]. mirror_coupling[s] equals mirror_coupling[s + 16].
All inputs are finite; a program needn't handle non-finite values.
Results may differ from the reference program's by a relative error of at most 0.0003.
Values sent between devices are 32-bit elements; how exact they have to be, the bound alone decides.
A program may use at most 64 MiB of HBM per device.

```python
import jax
import jax.numpy as jnp
from jax import lax

B = 128
TERMS_DEV = 24
S = 32
TERMS = 768
N_OPS = 32


def paired_tables(key):
    keys = jax.random.split(jax.random.fold_in(key, 7), 6)
    half_terms = TERMS // 2
    orders = jax.vmap(lambda item: jax.random.permutation(item, S))(jax.random.split(keys[0], half_terms))
    level = jax.random.randint(keys[1], (S,), 1, 8)
    empty_sector = jax.random.randint(keys[2], (), 0, S)
    level = jnp.where(jnp.arange(S) == empty_sector, 0, level)
    trials = jax.random.randint(keys[3], (half_terms, S), 0, 8)
    active = (trials < level[None, :]) | (jnp.arange(half_terms)[:, None] == 0)
    inverse = jnp.argsort(orders, axis=1, stable=True).astype(jnp.int32)
    back_active = jnp.take_along_axis(active, inverse, axis=1)
    forward = jnp.where(active, orders, -1)
    backward = jnp.where(back_active, inverse, -1)
    source = jnp.stack([forward, backward], axis=1).reshape(TERMS, S).astype(jnp.int32)
    left_half = jax.random.normal(keys[4], (half_terms, S, B, B), jnp.float32) * (B * TERMS) ** (-0.5)
    left_back = jnp.swapaxes(left_half[jnp.arange(half_terms)[:, None], inverse], 2, 3)
    left = jnp.stack([left_half, left_back], axis=1).reshape(TERMS, S, B, B)
    right_half = jax.random.normal(keys[5], (half_terms, B, B), jnp.float32) * B ** (-0.5)
    right = jnp.stack([right_half, jnp.swapaxes(right_half, 1, 2)], axis=1).reshape(TERMS, B, B)
    return (source, left, right)


def draw_term_source(key, part):
    return paired_tables(key)[0]


def draw_left_env(key, part):
    return paired_tables(key)[1]


def draw_right_env(key, part):
    return paired_tables(key)[2]


def draw_mirror_coupling(key, part):
    half_values = jax.random.uniform(jax.random.fold_in(key, 11), (S // 2,), jnp.float32, 0.5, 1.5)
    return jnp.concatenate([half_values, half_values])


def shard_levels(rng, dims, cuts, least, top_value):
    gain, own = 1.0, jax.random.fold_in(rng, 6)
    for axis_at, blocks in cuts:
        heights = jnp.exp(jax.random.uniform(jax.random.fold_in(own, axis_at), (blocks,), jnp.float32, least / len(cuts), top_value / len(cuts)))
        gain = gain * jnp.repeat(heights, dims[axis_at] // blocks).reshape([-1 if axis == axis_at else 1 for axis in range(len(dims))])
    return gain


def noise(own_key, extent, deviation, reach, cuts=(), kind=jnp.bfloat16):
    array = jax.random.normal(own_key, extent, jnp.float32) * deviation
    if len(cuts) > 0:
        array = shard_levels(own_key, extent, cuts, -0.22, 0.18) * array
    return jnp.clip(array, min=-reach, max=reach).astype(kind)


def setup_inputs(seed: int = 0) -> dict:
    streams_of = jax.random.split(jax.random.key(seed), 7)
    wavefunction = noise(streams_of[0], (S, B, B), 1.0, 6.0, ((0, 16),), jnp.float32)
    hamiltonian_diag = noise(streams_of[1], (S, B, B), 1.0, 6.0, ((0, 16),), jnp.float32)
    mirror_coupling = draw_mirror_coupling(jax.random.fold_in(streams_of[6], 71), 0)
    left_env = draw_left_env(jax.random.fold_in(streams_of[6], 71), 0)
    right_env = draw_right_env(jax.random.fold_in(streams_of[6], 71), 0)
    term_source = draw_term_source(jax.random.fold_in(streams_of[6], 71), 0)
    return {"wavefunction": wavefunction, "hamiltonian_diag": hamiltonian_diag, "mirror_coupling": mirror_coupling, "left_env": left_env, "right_env": right_env, "term_source": term_source}


HIGH = lax.Precision.HIGHEST

def apply_hamiltonian(vector, left_env, right_env, term_source, mirror_coupling):
    sectors = vector.shape[0]
    partner = jnp.roll(vector, sectors // 2, axis=0)
    mirrored = mirror_coupling[:, None, None] * jnp.swapaxes(partner, 1, 2)
    left_groups = left_env.reshape(N_OPS, TERMS_DEV, sectors, B, B)
    right_groups = right_env.reshape(N_OPS, TERMS_DEV, B, B)
    source_groups = term_source.reshape(N_OPS, TERMS_DEV, sectors)

    def group_step(total, pieces):
        left_block, right_block, source_block = pieces
        picked = vector[jnp.maximum(source_block, 0).astype(jnp.int32)]
        picked = jnp.where((source_block >= 0)[:, :, None, None], picked, jnp.zeros_like(picked))
        inner = jnp.einsum('ksij,ksjl->ksil', left_block, picked, precision=HIGH)
        outer = jnp.einsum('ksil,kml->sim', inner, right_block, precision=HIGH)
        return (total + outer, None)
    total, _ = lax.scan(group_step, jnp.zeros_like(vector), (left_groups, right_groups, source_groups))
    return total + mirrored

def reference(wavefunction, hamiltonian_diag, mirror_coupling, left_env, right_env, term_source):
    sigma = apply_hamiltonian(wavefunction, left_env, right_env, term_source, mirror_coupling)
    norm_sq = jnp.sum(wavefunction * wavefunction)
    correlation = jnp.sum(wavefunction * sigma)
    scale = jnp.sqrt(norm_sq)
    unit = wavefunction / scale
    rayleigh = correlation / norm_sq
    resid = sigma / scale - rayleigh * unit
    offset = hamiltonian_diag - rayleigh
    correction = resid / (1.0 + offset * offset)
    along = jnp.sum(unit * correction)
    correction = correction - along * unit
    direction = correction / jnp.sqrt(jnp.sum(correction * correction))
    dir_sigma = apply_hamiltonian(direction, left_env, right_env, term_source, mirror_coupling)
    coupling = jnp.sum(direction * resid)
    curvature = jnp.sum(direction * dir_sigma)
    half_gap = 0.5 * (curvature - rayleigh)
    energy = 0.5 * (rayleigh + curvature) - jnp.sqrt(half_gap * half_gap + coupling * coupling)
    angle = 0.5 * jnp.arctan2(-coupling, half_gap)
    new_wave = jnp.cos(angle) * wavefunction + jnp.sin(angle) * scale * direction
    new_sigma = jnp.cos(angle) * sigma + jnp.sin(angle) * scale * dir_sigma
    return (new_wave, new_sigma, jnp.reshape(energy, (1,)))
```

```python
import jax
import jax.numpy as jnp
from jax import lax
from jax.experimental import pallas as pl
from jax.experimental.pallas import tpu as pltpu
from jax.sharding import PartitionSpec as P

F32, BF16 = jnp.float32, jnp.bfloat16
B = 128
K = 24
OPS, SEC = 32, 16
Y, X = 4, 4


def remote(src, dst, send, recv, **device):
    return pltpu.make_async_remote_copy(
        src_ref=src,
        dst_ref=dst,
        send_sem=send,
        recv_sem=recv,
        device_id=device,
        device_id_type=pl.DeviceIdType.MESH,
    )


def arrived(ref, sem):
    pltpu.make_async_copy(ref, ref, sem).wait()


def split(value):
    high = value.astype(BF16)
    return high, (value - high.astype(F32)).astype(BF16)


def tile_sum(value):
    return jnp.sum(value.reshape(-1, 8, B), axis=0)


def total(value):
    return jnp.sum(jnp.sum(value, axis=0, keepdims=True), axis=1, keepdims=True)


def body(
    wave, diag, mirror, left, right, source,
    wave_out, sigma_out, energy_out,
    left_f32, right_f32, left2, right4, vec4, mid, part,
    whole, corr, diag_rows,
    msg, msg_in, tile_msg, rows_in, sib_in, msg2, msg2_in, curve_msg, curve_in,
    load_sem, a_send, a_recv, d_send, d_recv, g_send, g_recv, h_send, h_recv,
    p_send, p_recv, q_send, q_recv, s_send, s_recv, r_send, r_recv, e_send, e_recv,
):
    ops, sec = lax.axis_index("ops"), lax.axis_index("sec")
    core, chip = ops % 2, ops // 2
    y, x = chip // X, chip % X
    sibling = ops + 1 - 2 * core

    loads = [
        pltpu.make_async_copy(left, left_f32, load_sem.at[0]),
        pltpu.make_async_copy(right, right_f32, load_sem.at[1]),
    ]
    for load in loads:
        load.start()

    barrier = pltpu.get_barrier_semaphore()

    @pl.loop(1, OPS)
    def _(i):
        pl.semaphore_signal(
            barrier, inc=1, device_id={"ops": (ops + i) % OPS}, device_id_type=pl.DeviceIdType.MESH
        )

    @pl.loop(1, SEC)
    def _(i):
        pl.semaphore_signal(
            barrier, inc=1, device_id={"sec": (sec + i) % SEC}, device_id_type=pl.DeviceIdType.MESH
        )

    pl.semaphore_wait(barrier, OPS + SEC - 2)

    def to_sectors(src, dst, send, recv):
        pltpu.make_async_copy(src, dst.at[sec], recv).start()

        @pl.loop(1, SEC)
        def _(i):
            remote(src, dst.at[sec], send, recv, sec=(sec + i) % SEC).start()

    def to_ops(src, dst, send, recv):
        pltpu.make_async_copy(src.at[chip, core], dst.at[ops], recv).start()

        @pl.loop(1, OPS)
        def _(i):
            peer = (ops + i) % OPS
            remote(src.at[peer // 2, peer % 2], dst.at[ops], send, recv, ops=peer).start()

    def gather_ops(buf, send, recv):
        def chunk(row, column):
            return (row * X + column) * 2 + core

        def push(k, device):
            remote(buf.at[k], buf.at[k], send, recv.at[k], ops=device).start()

        rows = [y, y + 1 - 2 * (y % 2), y + 2 - 4 * (y // 2), 3 - y]
        near, far, opposite = (x + X - 1) % X, (x + 1) % X, (x + 2) % X

        def along_x(k):
            push(k, chunk(y, far))
            push(k, chunk(y, near))
            push(k, sibling)

        def column(i):
            for side, other, forward in ((near, far, i < 2), (far, near, i >= 2)):
                k = chunk(rows[i], side)
                arrived(buf.at[k], recv.at[k])
                if forward:
                    push(k, chunk(y, other))
                push(k, sibling)

        for i in (1, 2, 3):
            push(ops, chunk(rows[i], x))
        along_x(ops)
        for i in (1, 2, 3):
            k = chunk(rows[i], x)
            arrived(buf.at[k], recv.at[k])
            along_x(k)
            column(i - 1)
        column(3)
        for i in range(4):
            k = chunk(rows[i], opposite)
            arrived(buf.at[k], recv.at[k])
            push(k, sibling)

        @pl.loop(0, OPS // 2)
        def _(i):
            k = 2 * i + 1 - core
            arrived(buf.at[k], recv.at[k])

    def sector(buf, parity, pair):
        return buf.reshape(16, 2, buf.shape[1], 8, B)[:, parity, pair].reshape(B, B)

    def set_vec4(t, value):
        high, low = split(value)
        vec4[t, 0:B, 0:B] = high
        vec4[t, 0:B, B : 2 * B] = low
        vec4[t, B : 2 * B, 0:B] = low
        vec4[t, B : 2 * B, B : 2 * B] = high

    def contract(buf):
        @pl.loop(0, K)
        def _(k):
            for s in range(2):
                t = source[k, s]
                t = jnp.where(t < 0, 2 * SEC, t)
                both = jnp.dot(left2[k, s], vec4[t], preferred_element_type=F32)
                high, low = split(both[:, 0:B] + both[:, B : 2 * B])
                at = pl.multiple_of(k * 2 * B, 2 * B)
                mid[s * B : (s + 1) * B, pl.ds(at, B)] = high
                mid[s * B : (s + 1) * B, pl.ds(at + B, B)] = low

        both = jnp.dot(mid[...], right4[...], preferred_element_type=F32)
        inner = jnp.zeros((8, B), F32)
        for s in range(2):
            factor = jnp.where(ops == 0, mirror[s], jnp.float32(0.0))
            partner = sector(buf, s, (sec + SEC // 2) % SEC)
            rows = slice(s * B, (s + 1) * B)
            value = both[rows, 0:B] + both[rows, B : 2 * B] + factor * partner.T
            part[s] = value
            inner += tile_sum(value * sector(buf, s, sec))
        return jnp.sum(inner, axis=0, keepdims=True)

    mine = pl.ds(pl.multiple_of(chip * 8, 8), 8)
    to_sectors(wave.at[core, mine], whole.at[ops], a_send, a_recv)
    to_sectors(diag.at[core, mine], diag_rows, d_send, d_recv)

    for load in loads:
        load.wait()

    @pl.loop(0, K)
    def _(k):
        for s in range(2):
            high, low = split(left_f32[k, s])
            left2[k, s, :, 0:B] = high
            left2[k, s, :, B : 2 * B] = low
        high, low = split(right_f32[k + 1 - 2 * (k % 2)])
        at = pl.multiple_of(k * 2 * B, 2 * B)
        right4[pl.ds(at, B), 0:B] = high
        right4[pl.ds(at, B), B : 2 * B] = low
        right4[pl.ds(at + B, B), 0:B] = low
        right4[pl.ds(at + B, B), B : 2 * B] = high

    vec4[2 * SEC] = jnp.zeros((2 * B, 2 * B), BF16)

    arrived(whole.at[ops], a_recv)
    gather_ops(whole, g_send, g_recv)

    def convert(t, squares):
        value = sector(whole, t % 2, t // 2)
        set_vec4(t, value)
        return squares + tile_sum(value * value)

    norm_sq = total(lax.fori_loop(0, 2 * SEC, convert, jnp.zeros((8, B), F32)))
    scale = jnp.sqrt(norm_sq)

    inner = contract(whole)
    for s in range(2):
        msg[:, s, 0:8] = part[s].reshape(16, 8, B)
    msg[:, :, 8:9] = jnp.broadcast_to(inner[None, None], (OPS // 2, 2, 1, B))
    to_ops(msg, msg_in, p_send, p_recv)
    arrived(msg_in, p_recv)
    tile_msg[...] = jnp.sum(msg_in[...], axis=0)
    to_sectors(tile_msg, rows_in, q_send, q_recv)
    to_sibling = remote(tile_msg, sib_in, s_send, s_recv, ops=sibling)
    to_sibling.start()
    arrived(diag_rows, d_recv)
    arrived(rows_in, q_recv)

    correlation = jnp.sum(jnp.sum(rows_in[:, 8:9], axis=0), axis=1, keepdims=True)
    rayleigh = correlation / norm_sq
    unit = whole[ops] / scale
    resid = rows_in[:, 0:8] / scale - rayleigh * unit
    offset = diag_rows[...] - rayleigh
    correction = resid / (1.0 + offset * offset)
    corr[ops, 0:SEC] = correction
    sums = [unit * correction, correction * resid, unit * resid]
    sums = [jnp.sum(jnp.sum(v, axis=0), axis=0, keepdims=True) for v in sums]
    corr[ops, SEC] = jnp.concatenate([*sums, jnp.zeros((5, B), F32)], axis=0)
    gather_ops(corr, h_send, h_recv)

    sums = jnp.sum(jnp.sum(corr[:, SEC], axis=0), axis=1, keepdims=True)
    along, corr_resid, unit_resid = sums[0:1], sums[1:2], sums[2:3]
    by_scale = along / scale

    def subtract(t, squares):
        value = sector(corr, t % 2, t // 2) - by_scale * sector(whole, t % 2, t // 2)
        corr.reshape(16, 2, SEC + 1, 8, B)[:, t % 2, t // 2] = value.reshape(16, 8, B)
        set_vec4(t, value)
        return squares + tile_sum(value * value)

    arrived(corr.at[0 : OPS - 1], h_send)
    corr_sq = total(lax.fori_loop(0, 2 * SEC, subtract, jnp.zeros((8, B), F32)))
    length = jnp.sqrt(corr_sq)
    coupling = (corr_resid - along * unit_resid) / length

    inner = contract(corr)
    upper = lax.broadcasted_iota(jnp.int32, (16, 8, B), 1) < 4
    first, second = part[0].reshape(16, 8, B), part[1].reshape(16, 8, B)
    msg2[:, 0, 0:8] = jnp.where(upper, first, pltpu.roll(second, 4, 1))
    msg2[:, 1, 0:8] = jnp.where(upper, pltpu.roll(first, 4, 1), second)
    msg2[:, :, 8:9] = jnp.broadcast_to(inner[None, None], (OPS // 2, 2, 1, B))
    to_ops(msg2, msg2_in, r_send, r_recv)
    arrived(msg2_in, r_recv)
    summed = jnp.sum(msg2_in[...], axis=0)
    curve_msg[...] = summed[8:9]
    to_sectors(curve_msg, curve_in, e_send, e_recv)
    to_sibling.wait()

    def own(first, second):
        upper = lax.broadcasted_iota(jnp.int32, (8, B), 0) < 4
        top = jnp.where(upper, first, pltpu.roll(second, 4, 0))
        bottom = jnp.where(upper, pltpu.roll(first, 4, 0), second)
        return jnp.where(core == 0, top, bottom)

    def pair(buf):
        return own(buf[2 * chip, sec], buf[2 * chip + 1, sec])

    even = jnp.where(core == 0, tile_msg[0:8], sib_in[0:8])
    odd = jnp.where(core == 0, sib_in[0:8], tile_msg[0:8])
    sigma = own(even, odd)
    dir_sigma = summed[0:8] / length
    direction = pair(corr) / length
    wave_rows = pair(whole)

    arrived(curve_in, e_recv)
    curvature = jnp.sum(jnp.sum(curve_in[...], axis=0), axis=1, keepdims=True) / corr_sq
    half_gap = 0.5 * (curvature - rayleigh)
    root = jnp.sqrt(half_gap * half_gap + coupling * coupling)
    energy_out[...] = jnp.broadcast_to(0.5 * (rayleigh + curvature) - root, (1, B))
    safe = jnp.where(root > 0, root, 1.0)
    larger = jnp.sqrt(0.5 * (1.0 + jnp.abs(half_gap) / safe))
    smaller = 0.5 * jnp.abs(coupling) / (safe * larger)
    flat = half_gap >= 0
    cos_part = jnp.where(flat, larger, smaller)
    sin_part = jnp.where(flat, smaller, larger)
    sin_part = jnp.where(coupling >= 0, -sin_part, sin_part)
    cos_part = jnp.where(root > 0, cos_part, 1.0)
    sin_part = jnp.where(root > 0, sin_part, 0.0) * scale
    wave_out[...] = cos_part * wave_rows + sin_part * direction
    sigma_out[...] = cos_part * sigma + sin_part * dir_sigma

    arrived(whole.at[0, 0 : SEC - 1], a_send)
    arrived(diag_rows.at[0 : SEC - 1], d_send)
    arrived(whole.at[0 : OPS - 1], g_send)
    arrived(msg_in.at[0 : OPS - 1], p_send)
    arrived(rows_in.at[0 : SEC - 1], q_send)
    arrived(msg2_in.at[0 : OPS - 1], r_send)
    arrived(curve_in.at[0 : SEC - 1], e_send)


def step(wave, diag, mirror, left, right, source):
    dma = pltpu.SemaphoreType.DMA
    hbm = pl.BlockSpec(memory_space=pl.ANY)
    smem = pl.BlockSpec(memory_space=pltpu.SMEM)
    vmem = pl.BlockSpec(memory_space=pltpu.VMEM)
    wave_rows, sigma_rows, energy = pl.pallas_call(
        body,
        out_shape=(
            jax.ShapeDtypeStruct((8, B), F32),
            jax.ShapeDtypeStruct((8, B), F32),
            jax.ShapeDtypeStruct((1, B), F32),
        ),
        in_specs=[hbm, hbm, smem, hbm, hbm, smem],
        out_specs=(vmem, vmem, vmem),
        scratch_shapes=[
            pltpu.VMEM((K, 2, B, B), F32),
            pltpu.VMEM((K, B, B), F32),
            pltpu.VMEM((K, 2, B, 2 * B), BF16),
            pltpu.VMEM((K * 2 * B, 2 * B), BF16),
            pltpu.VMEM((2 * SEC + 1, 2 * B, 2 * B), BF16),
            pltpu.VMEM((2 * B, K * 2 * B), BF16),
            pltpu.VMEM((2, B, B), F32),
            pltpu.VMEM((OPS, SEC, 8, B), F32),
            pltpu.VMEM((OPS, SEC + 1, 8, B), F32),
            pltpu.VMEM((SEC, 8, B), F32),
            pltpu.VMEM((OPS // 2, 2, 9, B), F32),
            pltpu.VMEM((OPS, 9, B), F32),
            pltpu.VMEM((9, B), F32),
            pltpu.VMEM((SEC, 9, B), F32),
            pltpu.VMEM((9, B), F32),
            pltpu.VMEM((OPS // 2, 2, 9, B), F32),
            pltpu.VMEM((OPS, 9, B), F32),
            pltpu.VMEM((1, B), F32),
            pltpu.VMEM((SEC, 1, B), F32),
            dma((2,)),
            dma, dma, dma, dma,
            dma, dma((OPS,)), dma, dma((OPS,)),
            dma, dma, dma, dma, dma, dma, dma, dma, dma, dma,
        ],
        compiler_params=pltpu.CompilerParams(
            collective_id=0, has_side_effects=True, vmem_limit_bytes=48 * 2**20
        ),
        name="davidson_step",
    )(wave, diag, mirror, left, right, source)
    return (
        wave_rows.reshape(2, 4, B),
        sigma_rows.reshape(2, 4, B),
        energy[0, 0:1],
    )


def solution(mesh):
    return jax.shard_map(
        step,
        mesh=mesh,
        in_specs=(
            P("sec", None, None),
            P("sec", None, None),
            P("sec"),
            P("ops", "sec", None, None),
            P("ops", None, None),
            P("ops", "sec"),
        ),
        out_specs=(P("sec", "ops", None), P("sec", "ops", None), P()),
        check_vma=False,
    )
```

```python
import jax
import jax.numpy as jnp
from jax import lax
from jax.experimental import pallas as pl
from jax.experimental.pallas import tpu as pltpu
from jax.sharding import PartitionSpec as P

F32, BF16 = jnp.float32, jnp.bfloat16
B = 128
K = 24
OPS, SEC = 32, 16
X, Y, Z = 4, 8, 8
PLANE = 2 * OPS


def remote(src, dst, send, recv, device):
    return pltpu.make_async_remote_copy(
        src_ref=src,
        dst_ref=dst,
        send_sem=send,
        recv_sem=recv,
        device_id=device,
        device_id_type=pl.DeviceIdType.MESH,
    )


def arrived(ref, sem):
    pltpu.make_async_copy(ref, ref, sem).wait()


def split(value):
    high = value.astype(BF16)
    return high, (value - high.astype(F32)).astype(BF16)


def tile_sum(value):
    return jnp.sum(value.reshape(-1, 8, B), axis=0)


def total(value):
    return jnp.sum(jnp.sum(value, axis=0, keepdims=True), axis=1, keepdims=True)


def body(
    wave, diag, mirror, left, right, source,
    wave_out, sigma_out, energy_out,
    left_f32, right_f32, left2, right4, vec4, mid, part,
    whole, corr, diag_rows,
    msg, msg_in, sum_msg, sum_in, tile_msg, rows_in, sib_in,
    msg2, msg2_in, sum_msg2, sum2_in, curve_msg, curve_in,
    load_sem, a_send, a_recv, d_send, d_recv, g_send, g_recv, h_send, h_recv,
    p_send, p_recv, q_send, q_recv, s_send, s_recv, r_send, r_recv, e_send, e_recv,
    f_send, f_recv, c_send, c_recv,
):
    ops, sec = lax.axis_index("ops"), lax.axis_index("sec")
    core, chip = ops % 2, ops // 2
    x, half, z = chip % X, sec // Z, sec % Z
    y = half * (Y // 2) + chip // X
    me = half * OPS + ops

    def in_plane(k):
        return {"ops": k % OPS, "sec": k // OPS * Z + z}

    def along_z(i):
        return {"ops": ops, "sec": half * Z + (z + i) % Z}

    loads = [
        pltpu.make_async_copy(left, left_f32, load_sem.at[0]),
        pltpu.make_async_copy(right, right_f32, load_sem.at[1]),
    ]
    for load in loads:
        load.start()

    barrier = pltpu.get_barrier_semaphore()

    @pl.loop(1, PLANE)
    def _(i):
        pl.semaphore_signal(
            barrier, inc=1, device_id=in_plane((me + i) % PLANE), device_id_type=pl.DeviceIdType.MESH
        )

    @pl.loop(1, Z)
    def _(i):
        pl.semaphore_signal(
            barrier, inc=1, device_id=along_z(i), device_id_type=pl.DeviceIdType.MESH
        )

    for load in loads:
        load.wait()

    @pl.loop(0, K)
    def _(k):
        for s in range(2):
            high, low = split(left_f32[k, s])
            left2[k, s, :, 0:B] = high
            left2[k, s, :, B : 2 * B] = low
        high, low = split(right_f32[k + 1 - 2 * (k % 2)])
        at = pl.multiple_of(k * 2 * B, 2 * B)
        right4[pl.ds(at, B), 0:B] = high
        right4[pl.ds(at, B), B : 2 * B] = low
        right4[pl.ds(at + B, B), 0:B] = low
        right4[pl.ds(at + B, B), B : 2 * B] = high

    vec4[2 * SEC] = jnp.zeros((2 * B, 2 * B), BF16)
    pl.semaphore_wait(barrier, PLANE + Z - 2)
    leaving = []

    def to_z(src, dst, send, recv):
        pltpu.make_async_copy(src, dst.at[z], recv).start()

        @pl.loop(1, Z)
        def _(i):
            remote(src, dst.at[z], send, recv, along_z(i)).start()

        leaving.append((dst.at[0 : Z - 1], send))

    def to_ops(src, dst, send, recv):
        pltpu.make_async_copy(src.at[chip, core], dst.at[ops], recv).start()

        @pl.loop(1, OPS)
        def _(i):
            peer = (ops + i) % OPS
            there = {"ops": peer, "sec": sec}
            remote(src.at[peer // 2, peer % 2], dst.at[ops], send, recv, there).start()

        leaving.append((dst.at[0 : OPS - 1], send))

    def to_other_half(src, dst, send, recv):
        @pl.loop(0, OPS)
        def _(i):
            peer = (ops + i) % OPS
            there = {"ops": peer, "sec": (sec + Z) % SEC}
            remote(src, dst.at[ops], send, recv, there).start()

        leaving.append((dst, send))

    def gather_plane(buf, send, recv):
        def chunk(row, column, core):
            return (row * X + column) * 2 + core

        def push(k, device):
            remote(buf.at[k], buf.at[k], send, recv.at[k], in_plane(device)).start()

        def along_x(row):
            k = chunk(row, x, core)
            for i in (2, 1, 3):
                push(k, chunk(y, (x + i) % X, core))
            push(k, chunk(y, x, 1 - core))

        near_first = (1, 7, 2, 6, 3, 5, 4)
        for i in near_first:
            push(me, chunk((y + i) % Y, x, core))
        along_x(y)
        for i in near_first:
            row = (y + i) % Y
            k = chunk(row, x, core)
            arrived(buf.at[k], recv.at[k])
            along_x(row)
        for i in (0, *near_first):
            for column in (1, 3, 2):
                k = chunk((y + i) % Y, (x + column) % X, core)
                arrived(buf.at[k], recv.at[k])
                push(k, chunk(y, x, 1 - core))

        @pl.loop(0, PLANE // 2)
        def _(i):
            k = 2 * i + 1 - core
            arrived(buf.at[k], recv.at[k])

        return buf.at[0 : PLANE - 1], send

    def tiles(buf):
        return buf.reshape(2, 16, 2, buf.shape[1], 8, B)

    def sector(buf, t):
        pair = t // 2
        return tiles(buf)[pair // Z, :, t % 2, pair % Z].reshape(B, B)

    def set_vec4(t, value):
        high, low = split(value)
        vec4[t, 0:B, 0:B] = high
        vec4[t, 0:B, B : 2 * B] = low
        vec4[t, B : 2 * B, 0:B] = low
        vec4[t, B : 2 * B, B : 2 * B] = high

    def contract(buf):
        @pl.loop(0, K)
        def _(k):
            for s in range(2):
                t = source[s, k]
                t = jnp.where(t < 0, 2 * SEC, t)
                both = jnp.dot(left2[k, s], vec4[t], preferred_element_type=F32)
                high, low = split(both[:, 0:B] + both[:, B : 2 * B])
                at = pl.multiple_of(k * 2 * B, 2 * B)
                mid[s * B : (s + 1) * B, pl.ds(at, B)] = high
                mid[s * B : (s + 1) * B, pl.ds(at + B, B)] = low

        both = jnp.dot(mid[...], right4[...], preferred_element_type=F32)
        inner = jnp.zeros((8, B), F32)
        for s in range(2):
            factor = jnp.where(ops == 0, mirror[s], jnp.float32(0.0))
            partner = sector(buf, (2 * sec + s + SEC) % (2 * SEC))
            rows = slice(s * B, (s + 1) * B)
            value = both[rows, 0:B] + both[rows, B : 2 * B] + factor * partner.T
            part[s] = value
            inner += tile_sum(value * sector(buf, 2 * sec + s))
        return jnp.sum(inner, axis=0, keepdims=True)

    mine = pl.ds(pl.multiple_of(chip * 8, 8), 8)
    to_z(wave.at[core, mine], whole.at[me], a_send, a_recv)
    to_z(diag.at[core, mine], diag_rows, d_send, d_recv)
    arrived(whole.at[me], a_recv)
    leaving.append(gather_plane(whole, g_send, g_recv))

    def convert(t, squares):
        value = sector(whole, t)
        set_vec4(t, value)
        return squares + tile_sum(value * value)

    norm_sq = total(lax.fori_loop(0, 2 * SEC, convert, jnp.zeros((8, B), F32)))
    scale = jnp.sqrt(norm_sq)

    def either_half(mine, other_in):
        other = jnp.sum(other_in[...], axis=0)
        return jnp.where(half == 0, mine, other) + jnp.where(half == 0, other, mine)

    inner = contract(whole)
    for s in range(2):
        msg[:, s, 0:8] = part[s].reshape(16, 8, B)
    msg[:, :, 8:9] = jnp.broadcast_to(inner[None, None], (OPS // 2, 2, 1, B))
    sum_msg[...] = inner
    to_other_half(sum_msg, sum_in, f_send, f_recv)
    to_ops(msg, msg_in, p_send, p_recv)
    arrived(msg_in, p_recv)
    arrived(sum_in, f_recv)
    summed = jnp.sum(msg_in[...], axis=0)
    tile_msg[0:8] = summed[0:8]
    tile_msg[8:9] = either_half(summed[8:9], sum_in)
    to_z(tile_msg, rows_in, q_send, q_recv)
    to_sibling = remote(tile_msg, sib_in, s_send, s_recv, in_plane(me + 1 - 2 * core))
    to_sibling.start()
    arrived(diag_rows, d_recv)
    arrived(rows_in, q_recv)

    correlation = jnp.sum(jnp.sum(rows_in[:, 8:9], axis=0), axis=1, keepdims=True)
    rayleigh = correlation / norm_sq
    unit = whole[me] / scale
    resid = rows_in[:, 0:8] / scale - rayleigh * unit
    offset = diag_rows[...] - rayleigh
    correction = resid / (1.0 + offset * offset)
    corr[me, 0:Z] = correction
    sums = [unit * correction, correction * resid, unit * resid]
    sums = [jnp.sum(jnp.sum(v, axis=0), axis=0, keepdims=True) for v in sums]
    corr[me, Z] = jnp.concatenate([*sums, jnp.zeros((5, B), F32)], axis=0)
    sent = gather_plane(corr, h_send, h_recv)

    sums = jnp.sum(jnp.sum(corr[:, Z], axis=0), axis=1, keepdims=True)
    along, corr_resid, unit_resid = sums[0:1], sums[1:2], sums[2:3]
    by_scale = along / scale

    def subtract(t, squares):
        value = sector(corr, t) - by_scale * sector(whole, t)
        pair = t // 2
        tiles(corr)[pair // Z, :, t % 2, pair % Z] = value.reshape(16, 8, B)
        set_vec4(t, value)
        return squares + tile_sum(value * value)

    arrived(*sent)
    corr_sq = total(lax.fori_loop(0, 2 * SEC, subtract, jnp.zeros((8, B), F32)))
    length = jnp.sqrt(corr_sq)
    coupling = (corr_resid - along * unit_resid) / length

    inner = contract(corr)
    upper = lax.broadcasted_iota(jnp.int32, (16, 8, B), 1) < 4
    first, second = part[0].reshape(16, 8, B), part[1].reshape(16, 8, B)
    msg2[:, 0, 0:8] = jnp.where(upper, first, pltpu.roll(second, 4, 1))
    msg2[:, 1, 0:8] = jnp.where(upper, pltpu.roll(first, 4, 1), second)
    msg2[:, :, 8:9] = jnp.broadcast_to(inner[None, None], (OPS // 2, 2, 1, B))
    sum_msg2[...] = inner
    to_other_half(sum_msg2, sum2_in, c_send, c_recv)
    to_ops(msg2, msg2_in, r_send, r_recv)
    arrived(msg2_in, r_recv)
    arrived(sum2_in, c_recv)
    summed = jnp.sum(msg2_in[...], axis=0)
    curve_msg[...] = either_half(summed[8:9], sum2_in)
    to_z(curve_msg, curve_in, e_send, e_recv)
    to_sibling.wait()

    def own(first, second):
        upper = lax.broadcasted_iota(jnp.int32, (8, B), 0) < 4
        top = jnp.where(upper, first, pltpu.roll(second, 4, 0))
        bottom = jnp.where(upper, pltpu.roll(first, 4, 0), second)
        return jnp.where(core == 0, top, bottom)

    def pair(buf):
        return own(buf[me - core, z], buf[me - core + 1, z])

    even = jnp.where(core == 0, tile_msg[0:8], sib_in[0:8])
    odd = jnp.where(core == 0, sib_in[0:8], tile_msg[0:8])
    sigma = own(even, odd)
    dir_sigma = summed[0:8] / length
    direction = pair(corr) / length
    wave_rows = pair(whole)

    arrived(curve_in, e_recv)
    curvature = jnp.sum(jnp.sum(curve_in[...], axis=0), axis=1, keepdims=True) / corr_sq
    half_gap = 0.5 * (curvature - rayleigh)
    root = jnp.sqrt(half_gap * half_gap + coupling * coupling)
    energy_out[...] = jnp.broadcast_to(0.5 * (rayleigh + curvature) - root, (1, B))
    safe = jnp.where(root > 0, root, 1.0)
    larger = jnp.sqrt(0.5 * (1.0 + jnp.abs(half_gap) / safe))
    smaller = 0.5 * jnp.abs(coupling) / (safe * larger)
    flat = half_gap >= 0
    cos_part = jnp.where(flat, larger, smaller)
    sin_part = jnp.where(flat, smaller, larger)
    sin_part = jnp.where(coupling >= 0, -sin_part, sin_part)
    cos_part = jnp.where(root > 0, cos_part, 1.0)
    sin_part = jnp.where(root > 0, sin_part, 0.0) * scale
    wave_out[...] = cos_part * wave_rows + sin_part * direction
    sigma_out[...] = cos_part * sigma + sin_part * dir_sigma

    for ref, sem in leaving:
        arrived(ref, sem)


def step(wave, diag, mirror, left, right, source):
    dma = pltpu.SemaphoreType.DMA
    hbm = pl.BlockSpec(memory_space=pltpu.HBM)
    smem = pl.BlockSpec(memory_space=pltpu.SMEM)
    vmem = pl.BlockSpec(memory_space=pltpu.VMEM)
    wave_rows, sigma_rows, energy = pl.pallas_call(
        body,
        out_shape=(
            jax.ShapeDtypeStruct((8, B), F32),
            jax.ShapeDtypeStruct((8, B), F32),
            jax.ShapeDtypeStruct((1, B), F32),
        ),
        in_specs=[hbm, hbm, smem, hbm, hbm, smem],
        out_specs=(vmem, vmem, vmem),
        scratch_shapes=[
            pltpu.VMEM((K, 2, B, B), F32),
            pltpu.VMEM((K, B, B), F32),
            pltpu.VMEM((K, 2, B, 2 * B), BF16),
            pltpu.VMEM((K * 2 * B, 2 * B), BF16),
            pltpu.VMEM((2 * SEC + 1, 2 * B, 2 * B), BF16),
            pltpu.VMEM((2 * B, K * 2 * B), BF16),
            pltpu.VMEM((2, B, B), F32),
            pltpu.VMEM((PLANE, Z, 8, B), F32),
            pltpu.VMEM((PLANE, Z + 1, 8, B), F32),
            pltpu.VMEM((Z, 8, B), F32),
            pltpu.VMEM((OPS // 2, 2, 9, B), F32),
            pltpu.VMEM((OPS, 9, B), F32),
            pltpu.VMEM((1, B), F32),
            pltpu.VMEM((OPS, 1, B), F32),
            pltpu.VMEM((9, B), F32),
            pltpu.VMEM((Z, 9, B), F32),
            pltpu.VMEM((9, B), F32),
            pltpu.VMEM((OPS // 2, 2, 9, B), F32),
            pltpu.VMEM((OPS, 9, B), F32),
            pltpu.VMEM((1, B), F32),
            pltpu.VMEM((OPS, 1, B), F32),
            pltpu.VMEM((1, B), F32),
            pltpu.VMEM((Z, 1, B), F32),
            dma((2,)),
            dma, dma, dma, dma,
            dma, dma((PLANE,)), dma, dma((PLANE,)),
            *[dma] * 14,
        ],
        compiler_params=pltpu.CompilerParams(
            collective_id=0, has_side_effects=True, vmem_limit_bytes=62 * 2**20
        ),
        name="davidson_step",
    )(wave, diag, mirror, left, right, source.T)
    return (
        wave_rows.reshape(2, 4, B),
        sigma_rows.reshape(2, 4, B),
        energy[0, 0:1],
    )


def solution(mesh):
    return jax.shard_map(
        step,
        mesh=mesh,
        in_specs=(
            P("sec", None, None),
            P("sec", None, None),
            P("sec"),
            P("ops", "sec", None, None),
            P("ops", None, None),
            P("ops", "sec"),
        ),
        out_specs=(P("sec", "ops", None), P("sec", "ops", None), P()),
        check_vma=False,
    )
```

```python
import jax
import jax.numpy as jnp
from jax import lax
from jax.experimental import pallas as pl
from jax.experimental.pallas import tpu as pltpu
from jax.sharding import PartitionSpec as P

F32, BF16 = jnp.float32, jnp.bfloat16
B = 128
K = 24
OPS, SEC = 32, 16
X, Y, Z = 4, 8, 8
PLANE = 2 * OPS


def remote(src, dst, send, recv, device):
    return pltpu.make_async_remote_copy(
        src_ref=src,
        dst_ref=dst,
        send_sem=send,
        recv_sem=recv,
        device_id=device,
        device_id_type=pl.DeviceIdType.MESH,
    )


def arrived(ref, sem):
    pltpu.make_async_copy(ref, ref, sem).wait()


def split(value):
    high = value.astype(BF16)
    return high, (value - high.astype(F32)).astype(BF16)


def tile_sum(value):
    return jnp.sum(value.reshape(-1, 8, B), axis=0)


def total(value):
    return jnp.sum(jnp.sum(value, axis=0, keepdims=True), axis=1, keepdims=True)


def body(
    wave, diag, mirror, left, right, source,
    wave_out, sigma_out, energy_out,
    left_f32, right_f32, left2, right4, vec4, mid, part,
    whole, corr, diag_rows,
    msg, msg_in, sum_msg, sum_in, tile_msg, rows_in, sib_in,
    msg2, msg2_in, sum_msg2, sum2_in, curve_msg, curve_in,
    load_sem, a_send, a_recv, d_send, d_recv, g_send, g_recv, h_send, h_recv,
    p_send, p_recv, q_send, q_recv, s_send, s_recv, r_send, r_recv, e_send, e_recv,
    f_send, f_recv, c_send, c_recv,
):
    ops, sec = lax.axis_index("ops"), lax.axis_index("sec")
    core, chip = ops % 2, ops // 2
    x, half, z = chip % X, sec // Z, sec % Z
    y = half * (Y // 2) + chip // X
    me = half * OPS + ops

    def in_plane(k):
        return {"ops": k % OPS, "sec": k // OPS * Z + z}

    def along_z(i):
        return {"ops": ops, "sec": half * Z + (z + i) % Z}

    loads = [
        pltpu.make_async_copy(left, left_f32, load_sem.at[0]),
        pltpu.make_async_copy(right, right_f32, load_sem.at[1]),
    ]
    for load in loads:
        load.start()

    barrier = pltpu.get_barrier_semaphore()

    @pl.loop(1, PLANE)
    def _(i):
        pl.semaphore_signal(
            barrier, inc=1, device_id=in_plane((me + i) % PLANE), device_id_type=pl.DeviceIdType.MESH
        )

    @pl.loop(1, Z)
    def _(i):
        pl.semaphore_signal(
            barrier, inc=1, device_id=along_z(i), device_id_type=pl.DeviceIdType.MESH
        )

    for load in loads:
        load.wait()

    @pl.loop(0, K)
    def _(k):
        for s in range(2):
            high, low = split(left_f32[k, s])
            left2[k, s, :, 0:B] = high
            left2[k, s, :, B : 2 * B] = low
        high, low = split(right_f32[k + 1 - 2 * (k % 2)])
        at = pl.multiple_of(k * 2 * B, 2 * B)
        right4[pl.ds(at, B), 0:B] = high
        right4[pl.ds(at, B), B : 2 * B] = low
        right4[pl.ds(at + B, B), 0:B] = low
        right4[pl.ds(at + B, B), B : 2 * B] = high

    vec4[2 * SEC] = jnp.zeros((2 * B, 2 * B), BF16)
    pl.semaphore_wait(barrier, PLANE + Z - 2)
    leaving = []

    def to_z(src, dst, send, recv):
        pltpu.make_async_copy(src, dst.at[z], recv).start()

        @pl.loop(1, Z)
        def _(i):
            remote(src, dst.at[z], send, recv, along_z(i)).start()

        leaving.append((dst.at[0 : Z - 1], send))

    def to_ops(src, dst, send, recv):
        pltpu.make_async_copy(src.at[chip, core], dst.at[ops], recv).start()

        @pl.loop(1, OPS)
        def _(i):
            peer = (ops + i) % OPS
            there = {"ops": peer, "sec": sec}
            remote(src.at[peer // 2, peer % 2], dst.at[ops], send, recv, there).start()

        leaving.append((dst.at[0 : OPS - 1], send))

    def to_other_half(src, dst, send, recv):
        @pl.loop(0, OPS)
        def _(i):
            peer = (ops + i) % OPS
            there = {"ops": peer, "sec": (sec + Z) % SEC}
            remote(src, dst.at[ops], send, recv, there).start()

        leaving.append((dst, send))

    def gather_plane(buf, send, recv):
        def chunk(row, column, core):
            return (row * X + column) * 2 + core

        def push(k, device):
            remote(buf.at[k], buf.at[k], send, recv.at[k], in_plane(device)).start()

        def along_x(row):
            k = chunk(row, x, core)
            for i in (2, 1, 3):
                push(k, chunk(y, (x + i) % X, core))
            push(k, chunk(y, x, 1 - core))

        near_first = (1, 7, 2, 6, 3, 5, 4)
        for i in near_first:
            push(me, chunk((y + i) % Y, x, core))
        along_x(y)
        for i in near_first:
            row = (y + i) % Y
            k = chunk(row, x, core)
            arrived(buf.at[k], recv.at[k])
            along_x(row)
        for i in (0, *near_first):
            for column in (1, 3, 2):
                k = chunk((y + i) % Y, (x + column) % X, core)
                arrived(buf.at[k], recv.at[k])
                push(k, chunk(y, x, 1 - core))

        @pl.loop(0, PLANE // 2)
        def _(i):
            k = 2 * i + 1 - core
            arrived(buf.at[k], recv.at[k])

        return buf.at[0 : PLANE - 1], send

    def tiles(buf):
        return buf.reshape(2, 16, 2, buf.shape[1], 8, B)

    def sector(buf, t):
        pair = t // 2
        return tiles(buf)[pair // Z, :, t % 2, pair % Z].reshape(B, B)

    def set_vec4(t, value):
        high, low = split(value)
        vec4[t, 0:B, 0:B] = high
        vec4[t, 0:B, B : 2 * B] = low
        vec4[t, B : 2 * B, 0:B] = low
        vec4[t, B : 2 * B, B : 2 * B] = high

    def contract(buf):
        def first(k, carry):
            for s in range(2):
                t = source[s, k]
                t = jnp.where(t < 0, 2 * SEC, t)
                both = jnp.dot(left2[k, s], vec4[t], preferred_element_type=F32)
                high, low = split(both[:, 0:B] + both[:, B : 2 * B])
                at = pl.multiple_of(k * 2 * B, 2 * B)
                mid[s * B : (s + 1) * B, pl.ds(at, B)] = high
                mid[s * B : (s + 1) * B, pl.ds(at + B, B)] = low
            return carry

        lax.fori_loop(0, K, first, 0, unroll=8)

        both = jnp.dot(mid[...], right4[...], preferred_element_type=F32)
        inner = jnp.zeros((8, B), F32)
        for s in range(2):
            factor = jnp.where(ops == 0, mirror[s], jnp.float32(0.0))
            partner = sector(buf, (2 * sec + s + SEC) % (2 * SEC))
            rows = slice(s * B, (s + 1) * B)
            value = both[rows, 0:B] + both[rows, B : 2 * B] + factor * partner.T
            part[s] = value
            inner += tile_sum(value * sector(buf, 2 * sec + s))
        return jnp.sum(inner, axis=0, keepdims=True)

    mine = pl.ds(pl.multiple_of(chip * 8, 8), 8)
    to_z(wave.at[core, mine], whole.at[me], a_send, a_recv)
    to_z(diag.at[core, mine], diag_rows, d_send, d_recv)
    arrived(whole.at[me], a_recv)
    leaving.append(gather_plane(whole, g_send, g_recv))

    def convert(t, squares):
        value = sector(whole, t)
        set_vec4(t, value)
        return squares + tile_sum(value * value)

    norm_sq = total(lax.fori_loop(0, 2 * SEC, convert, jnp.zeros((8, B), F32)))
    scale = jnp.sqrt(norm_sq)

    def either_half(mine, other_in):
        other = jnp.sum(other_in[...], axis=0)
        return jnp.where(half == 0, mine, other) + jnp.where(half == 0, other, mine)

    inner = contract(whole)
    for s in range(2):
        msg[:, s, 0:8] = part[s].reshape(16, 8, B)
    msg[:, :, 8:9] = jnp.broadcast_to(inner[None, None], (OPS // 2, 2, 1, B))
    sum_msg[...] = inner
    to_other_half(sum_msg, sum_in, f_send, f_recv)
    to_ops(msg, msg_in, p_send, p_recv)
    arrived(msg_in, p_recv)
    arrived(sum_in, f_recv)
    summed = jnp.sum(msg_in[...], axis=0)
    tile_msg[0:8] = summed[0:8]
    tile_msg[8:9] = either_half(summed[8:9], sum_in)
    to_z(tile_msg, rows_in, q_send, q_recv)
    to_sibling = remote(tile_msg, sib_in, s_send, s_recv, in_plane(me + 1 - 2 * core))
    to_sibling.start()
    arrived(diag_rows, d_recv)
    arrived(rows_in, q_recv)

    correlation = jnp.sum(jnp.sum(rows_in[:, 8:9], axis=0), axis=1, keepdims=True)
    rayleigh = correlation / norm_sq
    unit = whole[me] / scale
    resid = rows_in[:, 0:8] / scale - rayleigh * unit
    offset = diag_rows[...] - rayleigh
    correction = resid / (1.0 + offset * offset)
    corr[me, 0:Z] = correction
    sums = [unit * correction, correction * resid, unit * resid]
    sums = [jnp.sum(jnp.sum(v, axis=0), axis=0, keepdims=True) for v in sums]
    corr[me, Z] = jnp.concatenate([*sums, jnp.zeros((5, B), F32)], axis=0)
    sent = gather_plane(corr, h_send, h_recv)

    sums = jnp.sum(jnp.sum(corr[:, Z], axis=0), axis=1, keepdims=True)
    along, corr_resid, unit_resid = sums[0:1], sums[1:2], sums[2:3]
    by_scale = along / scale

    def subtract(t, squares):
        value = sector(corr, t) - by_scale * sector(whole, t)
        pair = t // 2
        tiles(corr)[pair // Z, :, t % 2, pair % Z] = value.reshape(16, 8, B)
        set_vec4(t, value)
        return squares + tile_sum(value * value)

    arrived(*sent)
    corr_sq = total(lax.fori_loop(0, 2 * SEC, subtract, jnp.zeros((8, B), F32)))
    length = jnp.sqrt(corr_sq)
    coupling = (corr_resid - along * unit_resid) / length

    inner = contract(corr)
    upper = lax.broadcasted_iota(jnp.int32, (16, 8, B), 1) < 4
    first, second = part[0].reshape(16, 8, B), part[1].reshape(16, 8, B)
    msg2[:, 0, 0:8] = jnp.where(upper, first, pltpu.roll(second, 4, 1))
    msg2[:, 1, 0:8] = jnp.where(upper, pltpu.roll(first, 4, 1), second)
    msg2[:, :, 8:9] = jnp.broadcast_to(inner[None, None], (OPS // 2, 2, 1, B))
    sum_msg2[...] = inner
    to_other_half(sum_msg2, sum2_in, c_send, c_recv)
    to_ops(msg2, msg2_in, r_send, r_recv)
    arrived(msg2_in, r_recv)
    arrived(sum2_in, c_recv)
    summed = jnp.sum(msg2_in[...], axis=0)
    curve_msg[...] = either_half(summed[8:9], sum2_in)
    to_z(curve_msg, curve_in, e_send, e_recv)
    to_sibling.wait()

    def own(first, second):
        upper = lax.broadcasted_iota(jnp.int32, (8, B), 0) < 4
        top = jnp.where(upper, first, pltpu.roll(second, 4, 0))
        bottom = jnp.where(upper, pltpu.roll(first, 4, 0), second)
        return jnp.where(core == 0, top, bottom)

    def pair(buf):
        return own(buf[me - core, z], buf[me - core + 1, z])

    even = jnp.where(core == 0, tile_msg[0:8], sib_in[0:8])
    odd = jnp.where(core == 0, sib_in[0:8], tile_msg[0:8])
    sigma = own(even, odd)
    dir_sigma = summed[0:8] / length
    direction = pair(corr) / length
    wave_rows = pair(whole)

    arrived(curve_in, e_recv)
    curvature = jnp.sum(jnp.sum(curve_in[...], axis=0), axis=1, keepdims=True) / corr_sq
    half_gap = 0.5 * (curvature - rayleigh)
    root = jnp.sqrt(half_gap * half_gap + coupling * coupling)
    energy_out[...] = jnp.broadcast_to(0.5 * (rayleigh + curvature) - root, (1, B))
    safe = jnp.where(root > 0, root, 1.0)
    larger = jnp.sqrt(0.5 * (1.0 + jnp.abs(half_gap) / safe))
    smaller = 0.5 * jnp.abs(coupling) / (safe * larger)
    flat = half_gap >= 0
    cos_part = jnp.where(flat, larger, smaller)
    sin_part = jnp.where(flat, smaller, larger)
    sin_part = jnp.where(coupling >= 0, -sin_part, sin_part)
    cos_part = jnp.where(root > 0, cos_part, 1.0)
    sin_part = jnp.where(root > 0, sin_part, 0.0) * scale
    wave_out[...] = cos_part * wave_rows + sin_part * direction
    sigma_out[...] = cos_part * sigma + sin_part * dir_sigma

    for ref, sem in leaving:
        arrived(ref, sem)


def step(wave, diag, mirror, left, right, source):
    dma = pltpu.SemaphoreType.DMA
    hbm = pl.BlockSpec(memory_space=pltpu.HBM)
    smem = pl.BlockSpec(memory_space=pltpu.SMEM)
    vmem = pl.BlockSpec(memory_space=pltpu.VMEM)
    wave_rows, sigma_rows, energy = pl.pallas_call(
        body,
        out_shape=(
            jax.ShapeDtypeStruct((8, B), F32),
            jax.ShapeDtypeStruct((8, B), F32),
            jax.ShapeDtypeStruct((1, B), F32),
        ),
        in_specs=[hbm, hbm, smem, hbm, hbm, smem],
        out_specs=(vmem, vmem, vmem),
        scratch_shapes=[
            pltpu.VMEM((K, 2, B, B), F32),
            pltpu.VMEM((K, B, B), F32),
            pltpu.VMEM((K, 2, B, 2 * B), BF16),
            pltpu.VMEM((K * 2 * B, 2 * B), BF16),
            pltpu.VMEM((2 * SEC + 1, 2 * B, 2 * B), BF16),
            pltpu.VMEM((2 * B, K * 2 * B), BF16),
            pltpu.VMEM((2, B, B), F32),
            pltpu.VMEM((PLANE, Z, 8, B), F32),
            pltpu.VMEM((PLANE, Z + 1, 8, B), F32),
            pltpu.VMEM((Z, 8, B), F32),
            pltpu.VMEM((OPS // 2, 2, 9, B), F32),
            pltpu.VMEM((OPS, 9, B), F32),
            pltpu.VMEM((1, B), F32),
            pltpu.VMEM((OPS, 1, B), F32),
            pltpu.VMEM((9, B), F32),
            pltpu.VMEM((Z, 9, B), F32),
            pltpu.VMEM((9, B), F32),
            pltpu.VMEM((OPS // 2, 2, 9, B), F32),
            pltpu.VMEM((OPS, 9, B), F32),
            pltpu.VMEM((1, B), F32),
            pltpu.VMEM((OPS, 1, B), F32),
            pltpu.VMEM((1, B), F32),
            pltpu.VMEM((Z, 1, B), F32),
            dma((2,)),
            dma, dma, dma, dma,
            dma, dma((PLANE,)), dma, dma((PLANE,)),
            *[dma] * 14,
        ],
        compiler_params=pltpu.CompilerParams(
            collective_id=0, has_side_effects=True, vmem_limit_bytes=62 * 2**20
        ),
        name="davidson_step",
    )(wave, diag, mirror, left, right, source.T)
    return (
        wave_rows.reshape(2, 4, B),
        sigma_rows.reshape(2, 4, B),
        energy[0, 0:1],
    )


def solution(mesh):
    return jax.shard_map(
        step,
        mesh=mesh,
        in_specs=(
            P("sec", None, None),
            P("sec", None, None),
            P("sec"),
            P("ops", "sec", None, None),
            P("ops", None, None),
            P("ops", "sec"),
        ),
        out_specs=(P("sec", "ops", None), P("sec", "ops", None), P()),
        check_vma=False,
    )
```

```python
import jax
import jax.numpy as jnp
from jax import lax
from jax.experimental import pallas as pl
from jax.experimental.pallas import tpu as pltpu
from jax.sharding import PartitionSpec as P

F32, BF16 = jnp.float32, jnp.bfloat16
B = 128
K = 24
OPS, SEC = 32, 16
X, Y, Z = 4, 8, 8
PLANE = 2 * OPS


def remote(src, dst, send, recv, device):
    return pltpu.make_async_remote_copy(
        src_ref=src,
        dst_ref=dst,
        send_sem=send,
        recv_sem=recv,
        device_id=device,
        device_id_type=pl.DeviceIdType.MESH,
    )


def arrived(ref, sem):
    pltpu.make_async_copy(ref, ref, sem).wait()


def split(value):
    high = value.astype(BF16)
    return high, (value - high.astype(F32)).astype(BF16)


def tile_sum(value):
    return jnp.sum(value.reshape(-1, 8, B), axis=0)


def total(value):
    return jnp.sum(jnp.sum(value, axis=0, keepdims=True), axis=1, keepdims=True)


def body(
    wave, diag, mirror, left, right, source,
    out,
    left_f32, right_f32, left2, right4, vec4, mid, part,
    whole, corr, diag_rows,
    msg, msg_in, sum_msg, sum_in, tile_msg, rows_in, sib_in,
    msg2, msg2_in, sum_msg2, sum2_in, curve_msg, curve_in,
    load_sem, a_send, a_recv, d_send, d_recv, g_send, g_recv, h_send, h_recv,
    p_send, p_recv, q_send, q_recv, s_send, s_recv, r_send, r_recv, e_send, e_recv,
    f_send, f_recv, c_send, c_recv,
):
    ops, sec = lax.axis_index("ops"), lax.axis_index("sec")
    core, chip = ops % 2, ops // 2
    x, half, z = chip % X, sec // Z, sec % Z
    y = half * (Y // 2) + chip // X
    me = half * OPS + ops

    def in_plane(k):
        return {"ops": k % OPS, "sec": k // OPS * Z + z}

    def along_z(i):
        return {"ops": ops, "sec": half * Z + (z + i) % Z}

    loads = [
        pltpu.make_async_copy(left, left_f32, load_sem.at[0]),
        pltpu.make_async_copy(right, right_f32, load_sem.at[1]),
    ]
    for load in loads:
        load.start()

    barrier = pltpu.get_barrier_semaphore()

    @pl.loop(1, Z)
    def _(i):
        pl.semaphore_signal(
            barrier, inc=1, device_id=along_z(i), device_id_type=pl.DeviceIdType.MESH
        )

    @pl.loop(1, PLANE)
    def _(i):
        pl.semaphore_signal(
            barrier, inc=1, device_id=in_plane((me + i) % PLANE), device_id_type=pl.DeviceIdType.MESH
        )

    for load in loads:
        load.wait()

    @pl.loop(0, K)
    def _(k):
        for s in range(2):
            high, low = split(left_f32[k, s])
            left2[k, s, :, 0:B] = high
            left2[k, s, :, B : 2 * B] = low
        high, low = split(right_f32[k + 1 - 2 * (k % 2)])
        at = pl.multiple_of(k * 2 * B, 2 * B)
        right4[pl.ds(at, B), 0:B] = high
        right4[pl.ds(at, B), B : 2 * B] = low
        right4[pl.ds(at + B, B), 0:B] = low
        right4[pl.ds(at + B, B), B : 2 * B] = high

    vec4[2 * SEC] = jnp.zeros((2 * B, 2 * B), BF16)
    pl.semaphore_wait(barrier, PLANE + Z - 2)
    leaving = []

    def to_z(src, dst, send, recv):
        pltpu.make_async_copy(src, dst.at[z], recv).start()

        @pl.loop(1, Z)
        def _(i):
            remote(src, dst.at[z], send, recv, along_z(i)).start()

        leaving.append((dst.at[0 : Z - 1], send))

    def to_ops(src, dst, send, recv):
        pltpu.make_async_copy(src.at[chip, core], dst.at[ops], recv).start()

        @pl.loop(1, OPS)
        def _(i):
            peer = (ops + i) % OPS
            there = {"ops": peer, "sec": sec}
            remote(src.at[peer // 2, peer % 2], dst.at[ops], send, recv, there).start()

        leaving.append((dst.at[0 : OPS - 1], send))

    def to_other_half(src, dst, send, recv):
        @pl.loop(0, OPS)
        def _(i):
            peer = (ops + i) % OPS
            there = {"ops": peer, "sec": (sec + Z) % SEC}
            remote(src, dst.at[ops], send, recv, there).start()

        leaving.append((dst, send))

    def gather_plane(buf, send, recv):
        def chunk(row, column, core):
            return (row * X + column) * 2 + core

        def push(k, device):
            remote(buf.at[k], buf.at[k], send, recv.at[k], in_plane(device)).start()

        def along_x(row):
            k = chunk(row, x, core)
            for i in (2, 1, 3):
                push(k, chunk(y, (x + i) % X, core))
            push(k, chunk(y, x, 1 - core))

        near_first = (1, 7, 2, 6, 3, 5, 4)
        for i in near_first:
            push(me, chunk((y + i) % Y, x, core))
        along_x(y)
        for i in near_first:
            row = (y + i) % Y
            k = chunk(row, x, core)
            arrived(buf.at[k], recv.at[k])
            along_x(row)
        for i in (0, *near_first):
            for column in (1, 3, 2):
                k = chunk((y + i) % Y, (x + column) % X, core)
                arrived(buf.at[k], recv.at[k])
                push(k, chunk(y, x, 1 - core))

        @pl.loop(0, PLANE // 2)
        def _(i):
            k = 2 * i + 1 - core
            arrived(buf.at[k], recv.at[k])

        return buf.at[0 : PLANE - 1], send

    def tiles(buf):
        return buf.reshape(2, 16, 2, buf.shape[1], 8, B)

    def sector(buf, t):
        pair = t // 2
        return tiles(buf)[pair // Z, :, t % 2, pair % Z].reshape(B, B)

    def set_vec4(t, value):
        high, low = split(value)
        vec4[t, 0:B, 0:B] = high
        vec4[t, 0:B, B : 2 * B] = low
        vec4[t, B : 2 * B, 0:B] = low
        vec4[t, B : 2 * B, B : 2 * B] = high

    def contract(buf):
        def first(k, carry):
            for s in range(2):
                t = source[s, k]
                t = jnp.where(t < 0, 2 * SEC, t)
                both = jnp.dot(left2[k, s], vec4[t], preferred_element_type=F32)
                high, low = split(both[:, 0:B] + both[:, B : 2 * B])
                at = pl.multiple_of(k * 2 * B, 2 * B)
                mid[s * B : (s + 1) * B, pl.ds(at, B)] = high
                mid[s * B : (s + 1) * B, pl.ds(at + B, B)] = low
            return carry

        lax.fori_loop(0, K, first, 0, unroll=8)

        both = jnp.dot(mid[...], right4[...], preferred_element_type=F32)
        inner = jnp.zeros((8, B), F32)
        for s in range(2):
            factor = jnp.where(ops == 0, mirror[s], jnp.float32(0.0))
            partner = sector(buf, (2 * sec + s + SEC) % (2 * SEC))
            rows = slice(s * B, (s + 1) * B)
            value = both[rows, 0:B] + both[rows, B : 2 * B] + factor * partner.T
            part[s] = value
            inner += tile_sum(value * sector(buf, 2 * sec + s))
        return jnp.sum(inner, axis=0, keepdims=True)

    mine = pl.ds(pl.multiple_of(chip * 8, 8), 8)
    to_z(wave.at[core, mine], whole.at[me], a_send, a_recv)
    to_z(diag.at[core, mine], diag_rows, d_send, d_recv)
    arrived(whole.at[me], a_recv)
    leaving.append(gather_plane(whole, g_send, g_recv))

    def convert(t, squares):
        value = sector(whole, t)
        set_vec4(t, value)
        return squares + tile_sum(value * value)

    norm_sq = total(lax.fori_loop(0, 2 * SEC, convert, jnp.zeros((8, B), F32), unroll=4))
    scale = jnp.sqrt(norm_sq)

    def either_half(mine, other_in):
        other = jnp.sum(other_in[...], axis=0)
        return jnp.where(half == 0, mine, other) + jnp.where(half == 0, other, mine)

    inner = contract(whole)
    for s in range(2):
        msg[:, s, 0:8] = part[s].reshape(16, 8, B)
    msg[:, :, 8:9] = jnp.broadcast_to(inner[None, None], (OPS // 2, 2, 1, B))
    sum_msg[...] = inner
    to_other_half(sum_msg, sum_in, f_send, f_recv)
    to_ops(msg, msg_in, p_send, p_recv)
    arrived(msg_in, p_recv)
    arrived(sum_in, f_recv)
    summed = jnp.sum(msg_in[...], axis=0)
    tile_msg[0:8] = summed[0:8]
    tile_msg[8:9] = either_half(summed[8:9], sum_in)
    to_z(tile_msg, rows_in, q_send, q_recv)
    to_sibling = remote(tile_msg, sib_in, s_send, s_recv, in_plane(me + 1 - 2 * core))
    to_sibling.start()
    arrived(diag_rows, d_recv)
    arrived(rows_in, q_recv)

    correlation = jnp.sum(jnp.sum(rows_in[:, 8:9], axis=0), axis=1, keepdims=True)
    rayleigh = correlation / norm_sq
    unit = whole[me] / scale
    resid = rows_in[:, 0:8] / scale - rayleigh * unit
    offset = diag_rows[...] - rayleigh
    correction = resid / (1.0 + offset * offset)
    corr[me, 0:Z] = correction
    sums = [unit * correction, correction * resid, unit * resid]
    sums = [jnp.sum(jnp.sum(v, axis=0), axis=0, keepdims=True) for v in sums]
    corr[me, Z] = jnp.concatenate([*sums, jnp.zeros((5, B), F32)], axis=0)
    sent = gather_plane(corr, h_send, h_recv)

    sums = jnp.sum(jnp.sum(corr[:, Z], axis=0), axis=1, keepdims=True)
    along, corr_resid, unit_resid = sums[0:1], sums[1:2], sums[2:3]
    by_scale = along / scale

    def subtract(t, squares):
        value = sector(corr, t) - by_scale * sector(whole, t)
        pair = t // 2
        tiles(corr)[pair // Z, :, t % 2, pair % Z] = value.reshape(16, 8, B)
        set_vec4(t, value)
        return squares + tile_sum(value * value)

    arrived(*sent)
    corr_sq = total(lax.fori_loop(0, 2 * SEC, subtract, jnp.zeros((8, B), F32), unroll=4))
    length = jnp.sqrt(corr_sq)
    coupling = (corr_resid - along * unit_resid) / length

    inner = contract(corr)
    upper = lax.broadcasted_iota(jnp.int32, (16, 8, B), 1) < 4
    first, second = part[0].reshape(16, 8, B), part[1].reshape(16, 8, B)
    msg2[:, 0, 0:8] = jnp.where(upper, first, pltpu.roll(second, 4, 1))
    msg2[:, 1, 0:8] = jnp.where(upper, pltpu.roll(first, 4, 1), second)
    msg2[:, :, 8:9] = jnp.broadcast_to(inner[None, None], (OPS // 2, 2, 1, B))
    sum_msg2[...] = inner
    to_other_half(sum_msg2, sum2_in, c_send, c_recv)
    to_ops(msg2, msg2_in, r_send, r_recv)
    arrived(msg2_in, r_recv)
    arrived(sum2_in, c_recv)
    summed = jnp.sum(msg2_in[...], axis=0)
    curve_msg[...] = either_half(summed[8:9], sum2_in)
    to_z(curve_msg, curve_in, e_send, e_recv)
    to_sibling.wait()

    def own(first, second):
        upper = lax.broadcasted_iota(jnp.int32, (8, B), 0) < 4
        top = jnp.where(upper, first, pltpu.roll(second, 4, 0))
        bottom = jnp.where(upper, pltpu.roll(first, 4, 0), second)
        return jnp.where(core == 0, top, bottom)

    def pair(buf):
        return own(buf[me - core, z], buf[me - core + 1, z])

    even = jnp.where(core == 0, tile_msg[0:8], sib_in[0:8])
    odd = jnp.where(core == 0, sib_in[0:8], tile_msg[0:8])
    sigma = own(even, odd)
    dir_sigma = summed[0:8] / length
    direction = pair(corr) / length
    wave_rows = pair(whole)

    arrived(curve_in, e_recv)
    curvature = jnp.sum(jnp.sum(curve_in[...], axis=0), axis=1, keepdims=True) / corr_sq
    half_gap = 0.5 * (curvature - rayleigh)
    root = jnp.sqrt(half_gap * half_gap + coupling * coupling)
    out[16:24] = jnp.broadcast_to(0.5 * (rayleigh + curvature) - root, (8, B))
    safe = jnp.where(root > 0, root, 1.0)
    larger = jnp.sqrt(0.5 * (1.0 + jnp.abs(half_gap) / safe))
    smaller = 0.5 * jnp.abs(coupling) / (safe * larger)
    flat = half_gap >= 0
    cos_part = jnp.where(flat, larger, smaller)
    sin_part = jnp.where(flat, smaller, larger)
    sin_part = jnp.where(coupling >= 0, -sin_part, sin_part)
    cos_part = jnp.where(root > 0, cos_part, 1.0)
    sin_part = jnp.where(root > 0, sin_part, 0.0) * scale
    out[0:8] = cos_part * wave_rows + sin_part * direction
    out[8:16] = cos_part * sigma + sin_part * dir_sigma

    for ref, sem in leaving:
        arrived(ref, sem)


def step(wave, diag, mirror, left, right, source):
    dma = pltpu.SemaphoreType.DMA
    hbm = pl.BlockSpec(memory_space=pltpu.HBM)
    smem = pl.BlockSpec(memory_space=pltpu.SMEM)
    vmem = pl.BlockSpec(memory_space=pltpu.VMEM)
    out = pl.pallas_call(
        body,
        out_shape=jax.ShapeDtypeStruct((24, B), F32),
        in_specs=[hbm, hbm, smem, hbm, hbm, smem],
        out_specs=vmem,
        scratch_shapes=[
            pltpu.VMEM((K, 2, B, B), F32),
            pltpu.VMEM((K, B, B), F32),
            pltpu.VMEM((K, 2, B, 2 * B), BF16),
            pltpu.VMEM((K * 2 * B, 2 * B), BF16),
            pltpu.VMEM((2 * SEC + 1, 2 * B, 2 * B), BF16),
            pltpu.VMEM((2 * B, K * 2 * B), BF16),
            pltpu.VMEM((2, B, B), F32),
            pltpu.VMEM((PLANE, Z, 8, B), F32),
            pltpu.VMEM((PLANE, Z + 1, 8, B), F32),
            pltpu.VMEM((Z, 8, B), F32),
            pltpu.VMEM((OPS // 2, 2, 9, B), F32),
            pltpu.VMEM((OPS, 9, B), F32),
            pltpu.VMEM((1, B), F32),
            pltpu.VMEM((OPS, 1, B), F32),
            pltpu.VMEM((9, B), F32),
            pltpu.VMEM((Z, 9, B), F32),
            pltpu.VMEM((9, B), F32),
            pltpu.VMEM((OPS // 2, 2, 9, B), F32),
            pltpu.VMEM((OPS, 9, B), F32),
            pltpu.VMEM((1, B), F32),
            pltpu.VMEM((OPS, 1, B), F32),
            pltpu.VMEM((1, B), F32),
            pltpu.VMEM((Z, 1, B), F32),
            dma((2,)),
            dma, dma, dma, dma,
            dma, dma((PLANE,)), dma, dma((PLANE,)),
            *[dma] * 14,
        ],
        compiler_params=pltpu.CompilerParams(
            collective_id=0, has_side_effects=True, vmem_limit_bytes=62 * 2**20
        ),
        name="davidson_step",
    )(wave, diag, mirror, left, right, source.T)
    return out[0:8].reshape(2, 4, B), out[8:16].reshape(2, 4, B), out[16, 0:1]


def solution(mesh):
    return jax.shard_map(
        step,
        mesh=mesh,
        in_specs=(
            P("sec", None, None),
            P("sec", None, None),
            P("sec"),
            P("ops", "sec", None, None),
            P("ops", None, None),
            P("ops", "sec"),
        ),
        out_specs=(P("sec", "ops", None), P("sec", "ops", None), P()),
        check_vma=False,
    )
```

```python
import jax
import jax.numpy as jnp
from jax import lax
from jax.experimental import pallas as pl
from jax.experimental.pallas import tpu as pltpu
from jax.sharding import PartitionSpec as P

F32, BF16 = jnp.float32, jnp.bfloat16
B = 128
K = 24
OPS, SEC = 32, 16
X, Y, Z = 4, 8, 8
PLANE = 2 * OPS


def remote(src, dst, send, recv, device):
    return pltpu.make_async_remote_copy(
        src_ref=src,
        dst_ref=dst,
        send_sem=send,
        recv_sem=recv,
        device_id=device,
        device_id_type=pl.DeviceIdType.MESH,
    )


def arrived(ref, sem):
    pltpu.make_async_copy(ref, ref, sem).wait()


def split(value):
    high = value.astype(BF16)
    return high, (value - high.astype(F32)).astype(BF16)


def tile_sum(value):
    return jnp.sum(value.reshape(-1, 8, B), axis=0)


def total(value):
    return jnp.sum(jnp.sum(value, axis=0, keepdims=True), axis=1, keepdims=True)


def body(
    wave, diag, mirror, left, right, source,
    out,
    left_f32, right_f32, own_wave, own_diag, left2, right4, vec4, mid, part,
    whole, corr, diag_rows,
    msg, msg_in, sum_msg, sum_in, tile_msg, rows_in, sib_in,
    msg2, msg2_in, sum_msg2, sum2_in, curve_msg, curve_in,
    load_sem, a_send, a_recv, d_send, d_recv, g_send, g_recv, h_send, h_recv,
    p_send, p_recv, q_send, q_recv, s_send, s_recv, r_send, r_recv, e_send, e_recv,
    f_send, f_recv, c_send, c_recv,
):
    ops, sec = lax.axis_index("ops"), lax.axis_index("sec")
    core, chip = ops % 2, ops // 2
    x, half, z = chip % X, sec // Z, sec % Z
    y = half * (Y // 2) + chip // X
    me = half * OPS + ops

    def in_plane(k):
        return {"ops": k % OPS, "sec": k // OPS * Z + z}

    def along_z(i):
        return {"ops": ops, "sec": half * Z + (z + i) % Z}

    mine = pl.ds(pl.multiple_of(chip * 8, 8), 8)
    loads = [
        pltpu.make_async_copy(left, left_f32, load_sem.at[0]),
        pltpu.make_async_copy(right, right_f32, load_sem.at[1]),
        pltpu.make_async_copy(wave.at[core, mine], own_wave, load_sem.at[2]),
        pltpu.make_async_copy(diag.at[core, mine], own_diag, load_sem.at[3]),
    ]
    for load in loads:
        load.start()

    barrier = pltpu.get_barrier_semaphore()

    @pl.loop(1, Z)
    def _(i):
        pl.semaphore_signal(
            barrier, inc=1, device_id=along_z(i), device_id_type=pl.DeviceIdType.MESH
        )

    @pl.loop(1, PLANE)
    def _(i):
        pl.semaphore_signal(
            barrier, inc=1, device_id=in_plane((me + i) % PLANE), device_id_type=pl.DeviceIdType.MESH
        )

    for load in loads:
        load.wait()

    @pl.loop(0, K)
    def _(k):
        for s in range(2):
            high, low = split(left_f32[k, s])
            left2[k, s, :, 0:B] = high
            left2[k, s, :, B : 2 * B] = low
        high, low = split(right_f32[k + 1 - 2 * (k % 2)])
        at = pl.multiple_of(k * 2 * B, 2 * B)
        right4[pl.ds(at, B), 0:B] = high
        right4[pl.ds(at, B), B : 2 * B] = low
        right4[pl.ds(at + B, B), 0:B] = low
        right4[pl.ds(at + B, B), B : 2 * B] = high

    vec4[2 * SEC] = jnp.zeros((2 * B, 2 * B), BF16)
    pl.semaphore_wait(barrier, PLANE + Z - 2)
    leaving = []

    def to_z(src, dst, send, recv):
        pltpu.make_async_copy(src, dst.at[z], recv).start()

        @pl.loop(1, Z)
        def _(i):
            remote(src, dst.at[z], send, recv, along_z(i)).start()

        leaving.append((dst.at[0 : Z - 1], send))

    def to_ops(src, dst, send, recv):
        pltpu.make_async_copy(src.at[chip, core], dst.at[ops], recv).start()

        @pl.loop(1, OPS)
        def _(i):
            peer = (ops + i) % OPS
            there = {"ops": peer, "sec": sec}
            remote(src.at[peer // 2, peer % 2], dst.at[ops], send, recv, there).start()

        leaving.append((dst.at[0 : OPS - 1], send))

    def to_other_half(src, dst, send, recv):
        @pl.loop(0, OPS)
        def _(i):
            peer = (ops + i) % OPS
            there = {"ops": peer, "sec": (sec + Z) % SEC}
            remote(src, dst.at[ops], send, recv, there).start()

        leaving.append((dst, send))

    def gather_plane(buf, send, recv):
        def chunk(row, column, core):
            return (row * X + column) * 2 + core

        def push(k, device):
            remote(buf.at[k], buf.at[k], send, recv.at[k], in_plane(device)).start()

        def along_x(row):
            k = chunk(row, x, core)
            for i in (2, 1, 3):
                push(k, chunk(y, (x + i) % X, core))
            push(k, chunk(y, x, 1 - core))

        near_first = (1, 7, 2, 6, 3, 5, 4)
        for i in near_first:
            push(me, chunk((y + i) % Y, x, core))
        along_x(y)
        for i in near_first:
            row = (y + i) % Y
            k = chunk(row, x, core)
            arrived(buf.at[k], recv.at[k])
            along_x(row)
        for i in (0, *near_first):
            for column in (1, 3, 2):
                k = chunk((y + i) % Y, (x + column) % X, core)
                arrived(buf.at[k], recv.at[k])
                push(k, chunk(y, x, 1 - core))

        @pl.loop(0, PLANE // 2)
        def _(i):
            k = 2 * i + 1 - core
            arrived(buf.at[k], recv.at[k])

        return buf.at[0 : PLANE - 1], send

    def tiles(buf):
        return buf.reshape(2, 16, 2, buf.shape[1], 8, B)

    def sector(buf, t):
        pair = t // 2
        return tiles(buf)[pair // Z, :, t % 2, pair % Z].reshape(B, B)

    def set_vec4(t, value):
        high, low = split(value)
        vec4[t, 0:B, 0:B] = high
        vec4[t, 0:B, B : 2 * B] = low
        vec4[t, B : 2 * B, 0:B] = low
        vec4[t, B : 2 * B, B : 2 * B] = high

    def contract(buf):
        def first(k, carry):
            for s in range(2):
                t = source[s, k]
                t = jnp.where(t < 0, 2 * SEC, t)
                both = jnp.dot(left2[k, s], vec4[t], preferred_element_type=F32)
                high, low = split(both[:, 0:B] + both[:, B : 2 * B])
                at = pl.multiple_of(k * 2 * B, 2 * B)
                mid[s * B : (s + 1) * B, pl.ds(at, B)] = high
                mid[s * B : (s + 1) * B, pl.ds(at + B, B)] = low
            return carry

        lax.fori_loop(0, K, first, 0, unroll=8)

        both = jnp.dot(mid[...], right4[...], preferred_element_type=F32)
        inner = jnp.zeros((8, B), F32)
        for s in range(2):
            factor = jnp.where(ops == 0, mirror[s], jnp.float32(0.0))
            partner = sector(buf, (2 * sec + s + SEC) % (2 * SEC))
            rows = slice(s * B, (s + 1) * B)
            value = both[rows, 0:B] + both[rows, B : 2 * B] + factor * partner.T
            part[s] = value
            inner += tile_sum(value * sector(buf, 2 * sec + s))
        return jnp.sum(inner, axis=0, keepdims=True)

    to_z(own_wave, whole.at[me], a_send, a_recv)
    to_z(own_diag, diag_rows, d_send, d_recv)
    arrived(whole.at[me], a_recv)
    leaving.append(gather_plane(whole, g_send, g_recv))

    def convert(t, squares):
        value = sector(whole, t)
        set_vec4(t, value)
        return squares + tile_sum(value * value)

    norm_sq = total(lax.fori_loop(0, 2 * SEC, convert, jnp.zeros((8, B), F32), unroll=4))
    scale = jnp.sqrt(norm_sq)

    def either_half(mine, other_in):
        other = jnp.sum(other_in[...], axis=0)
        return jnp.where(half == 0, mine, other) + jnp.where(half == 0, other, mine)

    inner = contract(whole)
    for s in range(2):
        msg[:, s, 0:8] = part[s].reshape(16, 8, B)
    msg[:, :, 8:9] = jnp.broadcast_to(inner[None, None], (OPS // 2, 2, 1, B))
    sum_msg[...] = inner
    to_other_half(sum_msg, sum_in, f_send, f_recv)
    to_ops(msg, msg_in, p_send, p_recv)
    arrived(msg_in, p_recv)
    arrived(sum_in, f_recv)
    summed = jnp.sum(msg_in[...], axis=0)
    tile_msg[0:8] = summed[0:8]
    tile_msg[8:9] = either_half(summed[8:9], sum_in)
    to_z(tile_msg, rows_in, q_send, q_recv)
    to_sibling = remote(tile_msg, sib_in, s_send, s_recv, in_plane(me + 1 - 2 * core))
    to_sibling.start()
    arrived(diag_rows, d_recv)
    arrived(rows_in, q_recv)

    correlation = jnp.sum(jnp.sum(rows_in[:, 8:9], axis=0), axis=1, keepdims=True)
    rayleigh = correlation / norm_sq
    unit = whole[me] / scale
    resid = rows_in[:, 0:8] / scale - rayleigh * unit
    offset = diag_rows[...] - rayleigh
    correction = resid / (1.0 + offset * offset)
    corr[me, 0:Z] = correction
    sums = [unit * correction, correction * resid, unit * resid]
    sums = [jnp.sum(jnp.sum(v, axis=0), axis=0, keepdims=True) for v in sums]
    corr[me, Z] = jnp.concatenate([*sums, jnp.zeros((5, B), F32)], axis=0)
    sent = gather_plane(corr, h_send, h_recv)

    sums = jnp.sum(jnp.sum(corr[:, Z], axis=0), axis=1, keepdims=True)
    along, corr_resid, unit_resid = sums[0:1], sums[1:2], sums[2:3]
    by_scale = along / scale

    def subtract(t, squares):
        value = sector(corr, t) - by_scale * sector(whole, t)
        pair = t // 2
        tiles(corr)[pair // Z, :, t % 2, pair % Z] = value.reshape(16, 8, B)
        set_vec4(t, value)
        return squares + tile_sum(value * value)

    arrived(*sent)
    corr_sq = total(lax.fori_loop(0, 2 * SEC, subtract, jnp.zeros((8, B), F32), unroll=4))
    length = jnp.sqrt(corr_sq)
    coupling = (corr_resid - along * unit_resid) / length

    inner = contract(corr)
    upper = lax.broadcasted_iota(jnp.int32, (16, 8, B), 1) < 4
    first, second = part[0].reshape(16, 8, B), part[1].reshape(16, 8, B)
    msg2[:, 0, 0:8] = jnp.where(upper, first, pltpu.roll(second, 4, 1))
    msg2[:, 1, 0:8] = jnp.where(upper, pltpu.roll(first, 4, 1), second)
    msg2[:, :, 8:9] = jnp.broadcast_to(inner[None, None], (OPS // 2, 2, 1, B))
    sum_msg2[...] = inner
    to_other_half(sum_msg2, sum2_in, c_send, c_recv)
    to_ops(msg2, msg2_in, r_send, r_recv)
    arrived(msg2_in, r_recv)
    arrived(sum2_in, c_recv)
    summed = jnp.sum(msg2_in[...], axis=0)
    curve_msg[...] = either_half(summed[8:9], sum2_in)
    to_z(curve_msg, curve_in, e_send, e_recv)
    to_sibling.wait()

    def own(first, second):
        upper = lax.broadcasted_iota(jnp.int32, (8, B), 0) < 4
        top = jnp.where(upper, first, pltpu.roll(second, 4, 0))
        bottom = jnp.where(upper, pltpu.roll(first, 4, 0), second)
        return jnp.where(core == 0, top, bottom)

    def pair(buf):
        return own(buf[me - core, z], buf[me - core + 1, z])

    even = jnp.where(core == 0, tile_msg[0:8], sib_in[0:8])
    odd = jnp.where(core == 0, sib_in[0:8], tile_msg[0:8])
    sigma = own(even, odd)
    dir_sigma = summed[0:8] / length
    direction = pair(corr) / length
    wave_rows = pair(whole)

    arrived(curve_in, e_recv)
    curvature = jnp.sum(jnp.sum(curve_in[...], axis=0), axis=1, keepdims=True) / corr_sq
    half_gap = 0.5 * (curvature - rayleigh)
    root = jnp.sqrt(half_gap * half_gap + coupling * coupling)
    out[16:24] = jnp.broadcast_to(0.5 * (rayleigh + curvature) - root, (8, B))
    safe = jnp.where(root > 0, root, 1.0)
    larger = jnp.sqrt(0.5 * (1.0 + jnp.abs(half_gap) / safe))
    smaller = 0.5 * jnp.abs(coupling) / (safe * larger)
    flat = half_gap >= 0
    cos_part = jnp.where(flat, larger, smaller)
    sin_part = jnp.where(flat, smaller, larger)
    sin_part = jnp.where(coupling >= 0, -sin_part, sin_part)
    cos_part = jnp.where(root > 0, cos_part, 1.0)
    sin_part = jnp.where(root > 0, sin_part, 0.0) * scale
    out[0:8] = cos_part * wave_rows + sin_part * direction
    out[8:16] = cos_part * sigma + sin_part * dir_sigma

    for ref, sem in leaving:
        arrived(ref, sem)


def step(wave, diag, mirror, left, right, source):
    dma = pltpu.SemaphoreType.DMA
    hbm = pl.BlockSpec(memory_space=pltpu.HBM)
    smem = pl.BlockSpec(memory_space=pltpu.SMEM)
    vmem = pl.BlockSpec(memory_space=pltpu.VMEM)
    out = pl.pallas_call(
        body,
        out_shape=jax.ShapeDtypeStruct((24, B), F32),
        in_specs=[hbm, hbm, smem, hbm, hbm, smem],
        out_specs=vmem,
        scratch_shapes=[
            pltpu.VMEM((K, 2, B, B), F32),
            pltpu.VMEM((K, B, B), F32),
            pltpu.VMEM((8, B), F32),
            pltpu.VMEM((8, B), F32),
            pltpu.VMEM((K, 2, B, 2 * B), BF16),
            pltpu.VMEM((K * 2 * B, 2 * B), BF16),
            pltpu.VMEM((2 * SEC + 1, 2 * B, 2 * B), BF16),
            pltpu.VMEM((2 * B, K * 2 * B), BF16),
            pltpu.VMEM((2, B, B), F32),
            pltpu.VMEM((PLANE, Z, 8, B), F32),
            pltpu.VMEM((PLANE, Z + 1, 8, B), F32),
            pltpu.VMEM((Z, 8, B), F32),
            pltpu.VMEM((OPS // 2, 2, 9, B), F32),
            pltpu.VMEM((OPS, 9, B), F32),
            pltpu.VMEM((1, B), F32),
            pltpu.VMEM((OPS, 1, B), F32),
            pltpu.VMEM((9, B), F32),
            pltpu.VMEM((Z, 9, B), F32),
            pltpu.VMEM((9, B), F32),
            pltpu.VMEM((OPS // 2, 2, 9, B), F32),
            pltpu.VMEM((OPS, 9, B), F32),
            pltpu.VMEM((1, B), F32),
            pltpu.VMEM((OPS, 1, B), F32),
            pltpu.VMEM((1, B), F32),
            pltpu.VMEM((Z, 1, B), F32),
            dma((4,)),
            dma, dma, dma, dma,
            dma, dma((PLANE,)), dma, dma((PLANE,)),
            *[dma] * 14,
        ],
        compiler_params=pltpu.CompilerParams(
            collective_id=0, has_side_effects=True, vmem_limit_bytes=62 * 2**20
        ),
        name="davidson_step",
    )(wave, diag, mirror, left, right, source.T)
    return out[0:8].reshape(2, 4, B), out[8:16].reshape(2, 4, B), out[16, 0:1]


def solution(mesh):
    return jax.shard_map(
        step,
        mesh=mesh,
        in_specs=(
            P("sec", None, None),
            P("sec", None, None),
            P("sec"),
            P("ops", "sec", None, None),
            P("ops", None, None),
            P("ops", "sec"),
        ),
        out_specs=(P("sec", "ops", None), P("sec", "ops", None), P()),
        check_vma=False,
    )
```

```python
import jax
import jax.numpy as jnp
from jax import lax
from jax.experimental import pallas as pl
from jax.experimental.pallas import tpu as pltpu
from jax.sharding import PartitionSpec as P

F32, BF16 = jnp.float32, jnp.bfloat16
B = 128
K = 24
OPS, SEC = 32, 16
X, Y, Z = 4, 8, 8
PLANE = 2 * OPS


def remote(src, dst, send, recv, device):
    return pltpu.make_async_remote_copy(
        src_ref=src,
        dst_ref=dst,
        send_sem=send,
        recv_sem=recv,
        device_id=device,
        device_id_type=pl.DeviceIdType.MESH,
    )


def arrived(ref, sem):
    pltpu.make_async_copy(ref, ref, sem).wait()


def split(value):
    high = value.astype(BF16)
    return high, (value - high.astype(F32)).astype(BF16)


def tile_sum(value):
    return jnp.sum(value.reshape(-1, 8, B), axis=0)


def total(value):
    return jnp.sum(jnp.sum(value, axis=0, keepdims=True), axis=1, keepdims=True)


def body(
    wave, diag, mirror, left, right, source,
    out,
    left_f32, right_f32, own_wave, own_diag, left2, right4, vec4, mid, part,
    whole, corr, turned, diag_rows,
    msg, msg_in, sum_msg, sum_in, tile_msg, rows_in, sib_in,
    msg2, msg2_in, sum_msg2, sum2_in, curve_msg, curve_in,
    load_sem, a_send, a_recv, d_send, d_recv, g_send, g_recv, h_send, h_recv,
    p_send, p_recv, q_send, q_recv, s_send, s_recv, r_send, r_recv, e_send, e_recv,
    f_send, f_recv, c_send, c_recv,
):
    ops, sec = lax.axis_index("ops"), lax.axis_index("sec")
    core, chip = ops % 2, ops // 2
    x, half, z = chip % X, sec // Z, sec % Z
    y = half * (Y // 2) + chip // X
    me = half * OPS + ops

    def in_plane(k):
        return {"ops": k % OPS, "sec": k // OPS * Z + z}

    def along_z(i):
        return {"ops": ops, "sec": half * Z + (z + i) % Z}

    mine = pl.ds(pl.multiple_of(chip * 8, 8), 8)
    loads = [
        pltpu.make_async_copy(left, left_f32, load_sem.at[0]),
        pltpu.make_async_copy(right, right_f32, load_sem.at[1]),
        pltpu.make_async_copy(wave.at[core, mine], own_wave, load_sem.at[2]),
        pltpu.make_async_copy(diag.at[core, mine], own_diag, load_sem.at[3]),
    ]
    for load in loads:
        load.start()

    barrier = pltpu.get_barrier_semaphore()

    @pl.loop(1, Z)
    def _(i):
        pl.semaphore_signal(
            barrier, inc=1, device_id=along_z(i), device_id_type=pl.DeviceIdType.MESH
        )

    @pl.loop(1, PLANE)
    def _(i):
        pl.semaphore_signal(
            barrier, inc=1, device_id=in_plane((me + i) % PLANE), device_id_type=pl.DeviceIdType.MESH
        )

    for load in loads:
        load.wait()

    @pl.loop(0, K)
    def _(k):
        for s in range(2):
            high, low = split(left_f32[k, s])
            left2[k, s, :, 0:B] = high
            left2[k, s, :, B : 2 * B] = low
        high, low = split(right_f32[k + 1 - 2 * (k % 2)])
        at = pl.multiple_of(k * 2 * B, 2 * B)
        right4[pl.ds(at, B), 0:B] = high
        right4[pl.ds(at, B), B : 2 * B] = low
        right4[pl.ds(at + B, B), 0:B] = low
        right4[pl.ds(at + B, B), B : 2 * B] = high

    vec4[2 * SEC] = jnp.zeros((2 * B, 2 * B), BF16)
    pl.semaphore_wait(barrier, PLANE + Z - 2)
    leaving = []

    def to_z(src, dst, send, recv):
        pltpu.make_async_copy(src, dst.at[z], recv).start()

        @pl.loop(1, Z)
        def _(i):
            remote(src, dst.at[z], send, recv, along_z(i)).start()

        leaving.append((dst.at[0 : Z - 1], send))

    def to_ops(src, dst, send, recv):
        pltpu.make_async_copy(src.at[chip, core], dst.at[ops], recv).start()

        @pl.loop(1, OPS)
        def _(i):
            peer = (ops + i) % OPS
            there = {"ops": peer, "sec": sec}
            remote(src.at[peer // 2, peer % 2], dst.at[ops], send, recv, there).start()

        leaving.append((dst.at[0 : OPS - 1], send))

    def to_other_half(src, dst, send, recv):
        @pl.loop(0, OPS)
        def _(i):
            peer = (ops + i) % OPS
            there = {"ops": peer, "sec": (sec + Z) % SEC}
            remote(src, dst.at[ops], send, recv, there).start()

        leaving.append((dst, send))

    def gather_plane(buf, send, recv):
        def chunk(row, column, core):
            return (row * X + column) * 2 + core

        def push(k, device):
            remote(buf.at[k], buf.at[k], send, recv.at[k], in_plane(device)).start()

        def along_x(row):
            k = chunk(row, x, core)
            for i in (2, 1, 3):
                push(k, chunk(y, (x + i) % X, core))
            push(k, chunk(y, x, 1 - core))

        near_first = (1, 7, 2, 6, 3, 5, 4)
        for i in near_first:
            push(me, chunk((y + i) % Y, x, core))
        along_x(y)
        for i in near_first:
            row = (y + i) % Y
            k = chunk(row, x, core)
            arrived(buf.at[k], recv.at[k])
            along_x(row)
        for i in (0, *near_first):
            for column in (1, 3, 2):
                k = chunk((y + i) % Y, (x + column) % X, core)
                arrived(buf.at[k], recv.at[k])
                push(k, chunk(y, x, 1 - core))

        @pl.loop(0, PLANE // 2)
        def _(i):
            k = 2 * i + 1 - core
            arrived(buf.at[k], recv.at[k])

        return buf.at[0 : PLANE - 1], send

    def tiles(buf):
        return buf.reshape(2, 16, 2, buf.shape[1], 8, B)

    def sector(buf, t):
        pair = t // 2
        return tiles(buf)[pair // Z, :, t % 2, pair % Z].reshape(B, B)

    def set_vec4(t, value):
        high, low = split(value)
        vec4[t, 0:B, 0:B] = high
        vec4[t, 0:B, B : 2 * B] = low
        vec4[t, B : 2 * B, 0:B] = low
        vec4[t, B : 2 * B, B : 2 * B] = high

    def contract(buf):
        def first(k, carry):
            for s in range(2):
                t = source[s, k]
                t = jnp.where(t < 0, 2 * SEC, t)
                both = jnp.dot(left2[k, s], vec4[t], preferred_element_type=F32)
                high, low = split(both[:, 0:B] + both[:, B : 2 * B])
                at = pl.multiple_of(k * 2 * B, 2 * B)
                mid[s * B : (s + 1) * B, pl.ds(at, B)] = high
                mid[s * B : (s + 1) * B, pl.ds(at + B, B)] = low
            return carry

        lax.fori_loop(0, K, first, 0, unroll=8)

        both = jnp.dot(mid[...], right4[...], preferred_element_type=F32)
        inner = jnp.zeros((8, B), F32)
        for s in range(2):
            factor = jnp.where(ops == 0, mirror[s], jnp.float32(0.0))
            partner = sector(buf, (2 * sec + s + SEC) % (2 * SEC))
            rows = slice(s * B, (s + 1) * B)
            value = both[rows, 0:B] + both[rows, B : 2 * B] + factor * partner.T
            part[s] = value
            inner += tile_sum(value * sector(buf, 2 * sec + s))
        return jnp.sum(inner, axis=0, keepdims=True)

    to_z(own_wave, whole.at[me], a_send, a_recv)
    to_z(own_diag, diag_rows, d_send, d_recv)
    arrived(whole.at[me], a_recv)
    leaving.append(gather_plane(whole, g_send, g_recv))

    def convert(t, squares):
        value = sector(whole, t)
        set_vec4(t, value)
        return squares + tile_sum(value * value)

    norm_sq = total(lax.fori_loop(0, 2 * SEC, convert, jnp.zeros((8, B), F32), unroll=4))
    scale = jnp.sqrt(norm_sq)

    def either_half(mine, other_in):
        other = jnp.sum(other_in[...], axis=0)
        return jnp.where(half == 0, mine, other) + jnp.where(half == 0, other, mine)

    inner = contract(whole)
    for s in range(2):
        msg[:, s, 0:8] = part[s].reshape(16, 8, B)
    msg[:, :, 8:9] = jnp.broadcast_to(inner[None, None], (OPS // 2, 2, 1, B))
    sum_msg[...] = inner
    to_other_half(sum_msg, sum_in, f_send, f_recv)
    to_ops(msg, msg_in, p_send, p_recv)
    arrived(msg_in, p_recv)
    arrived(sum_in, f_recv)
    summed = jnp.sum(msg_in[...], axis=0)
    tile_msg[0:8] = summed[0:8]
    tile_msg[8:9] = either_half(summed[8:9], sum_in)
    to_z(tile_msg, rows_in, q_send, q_recv)
    to_sibling = remote(tile_msg, sib_in, s_send, s_recv, in_plane(me + 1 - 2 * core))
    to_sibling.start()
    arrived(diag_rows, d_recv)
    arrived(rows_in, q_recv)

    correlation = jnp.sum(jnp.sum(rows_in[:, 8:9], axis=0), axis=1, keepdims=True)
    rayleigh = correlation / norm_sq
    unit = whole[me] / scale
    resid = rows_in[:, 0:8] / scale - rayleigh * unit
    offset = diag_rows[...] - rayleigh
    correction = resid / (1.0 + offset * offset)
    corr[me, 0:Z] = correction
    sums = [unit * correction, correction * resid, unit * resid]
    sums = [jnp.sum(jnp.sum(v, axis=0), axis=0, keepdims=True) for v in sums]
    corr[me, Z] = jnp.concatenate([*sums, jnp.zeros((5, B), F32)], axis=0)
    leaving.append(gather_plane(corr, h_send, h_recv))

    sums = jnp.sum(jnp.sum(corr[:, Z], axis=0), axis=1, keepdims=True)
    along, corr_resid, unit_resid = sums[0:1], sums[1:2], sums[2:3]
    by_scale = along / scale

    def subtract(t, squares):
        value = sector(corr, t) - by_scale * sector(whole, t)
        pair = t // 2
        tiles(turned)[pair // Z, :, t % 2, pair % Z] = value.reshape(16, 8, B)
        set_vec4(t, value)
        return squares + tile_sum(value * value)

    corr_sq = total(lax.fori_loop(0, 2 * SEC, subtract, jnp.zeros((8, B), F32), unroll=4))
    length = jnp.sqrt(corr_sq)
    coupling = (corr_resid - along * unit_resid) / length

    inner = contract(turned)
    upper = lax.broadcasted_iota(jnp.int32, (16, 8, B), 1) < 4
    first, second = part[0].reshape(16, 8, B), part[1].reshape(16, 8, B)
    msg2[:, 0, 0:8] = jnp.where(upper, first, pltpu.roll(second, 4, 1))
    msg2[:, 1, 0:8] = jnp.where(upper, pltpu.roll(first, 4, 1), second)
    msg2[:, :, 8:9] = jnp.broadcast_to(inner[None, None], (OPS // 2, 2, 1, B))
    sum_msg2[...] = inner
    to_other_half(sum_msg2, sum2_in, c_send, c_recv)
    to_ops(msg2, msg2_in, r_send, r_recv)
    arrived(msg2_in, r_recv)
    arrived(sum2_in, c_recv)
    summed = jnp.sum(msg2_in[...], axis=0)
    curve_msg[...] = either_half(summed[8:9], sum2_in)
    to_z(curve_msg, curve_in, e_send, e_recv)
    to_sibling.wait()

    def own(first, second):
        upper = lax.broadcasted_iota(jnp.int32, (8, B), 0) < 4
        top = jnp.where(upper, first, pltpu.roll(second, 4, 0))
        bottom = jnp.where(upper, pltpu.roll(first, 4, 0), second)
        return jnp.where(core == 0, top, bottom)

    def pair(buf):
        return own(buf[me - core, z], buf[me - core + 1, z])

    even = jnp.where(core == 0, tile_msg[0:8], sib_in[0:8])
    odd = jnp.where(core == 0, sib_in[0:8], tile_msg[0:8])
    sigma = own(even, odd)
    dir_sigma = summed[0:8] / length
    direction = pair(turned) / length
    wave_rows = pair(whole)

    arrived(curve_in, e_recv)
    curvature = jnp.sum(jnp.sum(curve_in[...], axis=0), axis=1, keepdims=True) / corr_sq
    half_gap = 0.5 * (curvature - rayleigh)
    root = jnp.sqrt(half_gap * half_gap + coupling * coupling)
    out[16:24] = jnp.broadcast_to(0.5 * (rayleigh + curvature) - root, (8, B))
    safe = jnp.where(root > 0, root, 1.0)
    larger = jnp.sqrt(0.5 * (1.0 + jnp.abs(half_gap) / safe))
    smaller = 0.5 * jnp.abs(coupling) / (safe * larger)
    flat = half_gap >= 0
    cos_part = jnp.where(flat, larger, smaller)
    sin_part = jnp.where(flat, smaller, larger)
    sin_part = jnp.where(coupling >= 0, -sin_part, sin_part)
    cos_part = jnp.where(root > 0, cos_part, 1.0)
    sin_part = jnp.where(root > 0, sin_part, 0.0) * scale
    out[0:8] = cos_part * wave_rows + sin_part * direction
    out[8:16] = cos_part * sigma + sin_part * dir_sigma

    for ref, sem in leaving:
        arrived(ref, sem)


def step(wave, diag, mirror, left, right, source):
    dma = pltpu.SemaphoreType.DMA
    hbm = pl.BlockSpec(memory_space=pltpu.HBM)
    smem = pl.BlockSpec(memory_space=pltpu.SMEM)
    vmem = pl.BlockSpec(memory_space=pltpu.VMEM)
    out = pl.pallas_call(
        body,
        out_shape=jax.ShapeDtypeStruct((24, B), F32),
        in_specs=[hbm, hbm, smem, hbm, hbm, smem],
        out_specs=vmem,
        scratch_shapes=[
            pltpu.VMEM((K, 2, B, B), F32),
            pltpu.VMEM((K, B, B), F32),
            pltpu.VMEM((8, B), F32),
            pltpu.VMEM((8, B), F32),
            pltpu.VMEM((K, 2, B, 2 * B), BF16),
            pltpu.VMEM((K * 2 * B, 2 * B), BF16),
            pltpu.VMEM((2 * SEC + 1, 2 * B, 2 * B), BF16),
            pltpu.VMEM((2 * B, K * 2 * B), BF16),
            pltpu.VMEM((2, B, B), F32),
            pltpu.VMEM((PLANE, Z, 8, B), F32),
            pltpu.VMEM((PLANE, Z + 1, 8, B), F32),
            pltpu.VMEM((PLANE, Z, 8, B), F32),
            pltpu.VMEM((Z, 8, B), F32),
            pltpu.VMEM((OPS // 2, 2, 9, B), F32),
            pltpu.VMEM((OPS, 9, B), F32),
            pltpu.VMEM((1, B), F32),
            pltpu.VMEM((OPS, 1, B), F32),
            pltpu.VMEM((9, B), F32),
            pltpu.VMEM((Z, 9, B), F32),
            pltpu.VMEM((9, B), F32),
            pltpu.VMEM((OPS // 2, 2, 9, B), F32),
            pltpu.VMEM((OPS, 9, B), F32),
            pltpu.VMEM((1, B), F32),
            pltpu.VMEM((OPS, 1, B), F32),
            pltpu.VMEM((1, B), F32),
            pltpu.VMEM((Z, 1, B), F32),
            dma((4,)),
            dma, dma, dma, dma,
            dma, dma((PLANE,)), dma, dma((PLANE,)),
            *[dma] * 14,
        ],
        compiler_params=pltpu.CompilerParams(
            collective_id=0, has_side_effects=True, vmem_limit_bytes=62 * 2**20
        ),
        name="davidson_step",
    )(wave, diag, mirror, left, right, source.T)
    return out[0:8].reshape(2, 4, B), out[8:16].reshape(2, 4, B), out[16, 0:1]


def solution(mesh):
    return jax.shard_map(
        step,
        mesh=mesh,
        in_specs=(
            P("sec", None, None),
            P("sec", None, None),
            P("sec"),
            P("ops", "sec", None, None),
            P("ops", None, None),
            P("ops", "sec"),
        ),
        out_specs=(P("sec", "ops", None), P("sec", "ops", None), P()),
        check_vma=False,
    )
```
